256 devices in a mesh: span: 16 (over y_lo, z), chord: 4 (over x), normal: 4 (over y_hi, core).
Axes of the slice: x: 4, y: 4 (y_hi: 2, y_lo: 2; y = y_hi * 2 + y_lo), z: 8, core: 2. Of those that a mesh axis runs over, the one named last changes fastest.
Arguments:
- adjoint: float32 [5, 128, 32, 512], P(None, 'span', 'chord', 'normal'), may hold values from -6 to 6
- jacobian: bfloat16 [7, 5, 5, 128, 32, 512], P(None, None, None, 'span', 'chord', 'normal'), may hold values from -1 to 1
- wall_table: float32 [3, 5, 5], replicated, may hold values from -3 to 3
- face_type: int32 [128, 32], P('span', 'chord'), may hold values from 0 to 2
- mesh_map: float32 [3, 5], replicated, may hold values from -2.5 to 2.5
- stiffness: float32 [7, 128, 32, 512], P(None, 'span', 'chord', 'normal'), may hold values from 0.1 to 1
- box_map: int32 [16, 4, 4], P('span', 'chord', 'normal'), may hold values from 0 to 15
- offsets: int32 [16, 4, 4, 3], P('span', 'chord', 'normal'), may hold values from 0 to 88, as said below
Outputs:
- mesh_adjoint: float32 [3, 128, 32, 512], P(None, 'span', 'chord', 'normal')
- ffd_grad: float32 [16, 3, 49152], P('span', None, ('chord', 'normal'))
The draws below stay inside these ranges and needn't reach their ends.
Inputs may be any that keep to these rules, and one draw needn't show every extreme that they name: `offsets`: column 0 is at most 88, column 1 at most 24, column 2 at most 8, so every window lies inside its box.
All inputs are finite; a program needn't handle non-finite values.
Results may differ from the reference program's by a relative error of at most 0.0003.
Values sent between devices are 32-bit elements; how exact they have to be, the bound alone decides.
No kernel may reach another device: no remote copies, remote signals or barrier semaphores. Data moves between devices by JAX's collectives and lax.ppermute only.
A program may use at most 192 MiB of HBM per device.

```python
import math
import jax
import jax.numpy as jnp
import numpy as np
from jax import lax

CX = 8
CY = 8
CZ = 128
LA = 96
LB = 32
LC = 16
WA = 8
WB = 8
WC = 8
NX = 128
NY = 32
NZ = 512
NBOX = 16
CHORD_BLOCKS = 4
NORMAL_BLOCKS = 4
LAT = 49152


def draw_offsets(key, part):
    tops = jnp.array([LA - WA, LB - WB, LC - WC], jnp.int32)
    values = jax.random.randint(key, (NBOX, CHORD_BLOCKS, NORMAL_BLOCKS, 3), 0, tops + 1, dtype=jnp.int32)
    values = values.at[0, 0, 0].set(tops)
    values = values.at[NBOX - 1, CHORD_BLOCKS - 1, NORMAL_BLOCKS - 1].set(jnp.zeros((3,), jnp.int32))
    return values.astype(jnp.int32)


def plant(drawn, key, least, largest):
    longest = drawn.shape.index(max(drawn.shape))
    spots = []
    for shift in (0, 1):
        where = [jax.random.randint(jax.random.fold_in(key, axis), (), 0, length) for axis, length in enumerate(drawn.shape)]
        where[longest] = (where[longest] + shift) % drawn.shape[longest]
        spots.append(tuple(where))
    return drawn.at[spots[0]].set(least).at[spots[1]].set(largest)


def block_levels(key, dims, shards, smallest, top_value):
    gain = 1.0
    for position, blocks in shards:
        heights = jax.random.uniform(jax.random.fold_in(jax.random.fold_in(key, 6), position), (blocks,), jnp.float32, smallest / len(shards), top_value / len(shards))
        gain = gain * jnp.repeat(jnp.exp(heights), dims[position] // blocks).reshape((-1,) + (1,) * (len(dims) - 1 - position))
    return gain


def scatter_about(key, dims, deviation, reach, shards=(), kind=jnp.bfloat16):
    result = jax.random.normal(key, dims, jnp.float32) * deviation
    if len(shards) > 0:
        result = block_levels(key, dims, shards, -0.22, 0.18) * result
    return jnp.clip(result, min=-reach, max=reach).astype(kind)


def setup_inputs(seed: int = 0) -> dict:
    streams_of = jax.random.split(jax.random.key(seed), 9)
    adjoint = scatter_about(streams_of[0], (5, NX, NY, NZ), 1.0, 6.0, ((1, 16), (2, 4), (3, 4)), jnp.float32)
    jacobian = scatter_about(streams_of[1], (7, 5, 5, NX, NY, NZ), 35 ** -0.5, 1.0, ((3, 16), (4, 4), (5, 4)))
    wall_table = scatter_about(streams_of[2], (3, 5, 5), 0.5, 3.0, (), jnp.float32)
    face_type = plant(jax.random.randint(streams_of[3], (NX, NY), 0, 3), jax.random.fold_in(streams_of[3], 1), 0, 2).astype(jnp.int32)
    mesh_map = scatter_about(streams_of[4], (3, 5), 5 ** -0.5, 2.5, (), jnp.float32)
    stiffness = jnp.clip(jnp.exp(math.log(1.0) - 2.3025851 * jax.random.uniform(streams_of[5], (7, NX, NY, NZ), jnp.float32) ** block_levels(streams_of[5], (7, NX, NY, NZ), ((1, 16), (2, 4), (3, 4)), -0.2, 0.2)), 0.1, 1.0)
    box_map = plant(jax.random.randint(streams_of[6], (NBOX, CHORD_BLOCKS, NORMAL_BLOCKS), 0, NBOX), jax.random.fold_in(streams_of[6], 1), 0, NBOX - 1).astype(jnp.int32)
    offsets = draw_offsets(jax.random.fold_in(streams_of[8], 71), 0)
    return {"adjoint": adjoint, "jacobian": jacobian, "wall_table": wall_table, "face_type": face_type, "mesh_map": mesh_map, "stiffness": stiffness, "box_map": box_map, "offsets": offsets}


HIGHEST = lax.Precision.HIGHEST


def neighbours(padded):
    width_x = padded.shape[1] - 2
    width_y = padded.shape[2] - 2
    width_z = padded.shape[3] - 2

    def cut(step_x, step_y, step_z):
        return padded[:, 1 + step_x:1 + step_x + width_x, 1 + step_y:1 + step_y + width_y, 1 + step_z:1 + step_z + width_z]

    return [cut(0, 0, 0), cut(-1, 0, 0), cut(1, 0, 0), cut(0, -1, 0), cut(0, 1, 0), cut(0, 0, -1), cut(0, 0, 1)]


def flux_sweep(shifted, jacobian):
    total = jnp.zeros(jacobian.shape[2:], jnp.float32)
    for direction in range(7):
        for source in range(5):
            total = total + jacobian[direction, source].astype(jnp.float32) * shifted[direction][source][None]
    return total


def wall_term(adjoint_layer, face_type, wall_table):
    onehot = (face_type[None] == jnp.arange(3, dtype=jnp.int32)[:, None, None]).astype(jnp.float32)
    table = jnp.einsum('tpq,txy->pqxy', wall_table, onehot, precision=HIGHEST)
    return jnp.einsum('pqxy,pxy->qxy', table, adjoint_layer, precision=HIGHEST)


def elastic_apply(shifted, stiffness, diagonal):
    total = diagonal[None] * shifted[0]
    for direction in range(1, 7):
        total = total - stiffness[direction][None] * shifted[direction]
    return total


def bernstein(count, cells):
    degree = count - 1
    binomial = jnp.asarray(np.array([math.comb(degree, point) for point in range(count)]), dtype=jnp.float32)
    coords = (jnp.arange(cells, dtype=jnp.float32) + 0.5) / cells
    powers = jnp.arange(count, dtype=jnp.float32)
    return binomial[:, None] * coords[None, :] ** powers[:, None] * (1.0 - coords[None, :]) ** (degree - powers)[:, None]


def ffd_window(field):
    along_x = bernstein(WA, field.shape[1])
    along_y = bernstein(WB, field.shape[2])
    along_z = bernstein(WC, field.shape[3])
    inner = jnp.einsum('cxyz,gz->cxyg', field, along_z, precision=HIGHEST)
    inner = jnp.einsum('cxyg,by->cxbg', inner, along_y, precision=HIGHEST)
    return 8.0 * jnp.einsum('cxbg,ax->cabg', inner, along_x, precision=HIGHEST)


def pad_field(field):
    return jnp.pad(field, ((0, 0), (1, 1), (1, 1), (1, 1)))


def reference(adjoint, jacobian, wall_table, face_type, mesh_map, stiffness, box_map, offsets):
    residual = flux_sweep(neighbours(pad_field(adjoint)), jacobian)
    residual = residual.at[:, :, :, 0].add(wall_term(adjoint[:, :, :, 0], face_type, wall_table))
    sensitivity = jnp.einsum('rq,qxyz->rxyz', mesh_map, residual, precision=HIGHEST)
    diagonal = stiffness[0] + jnp.sum(stiffness[1:], axis=0)
    iterate = sensitivity / diagonal[None]
    for sweep in range(2):
        applied = elastic_apply(neighbours(pad_field(iterate)), stiffness, diagonal)
        iterate = iterate + (sensitivity - applied) / diagonal[None]
    mesh_adjoint = iterate
    zero = jnp.zeros((), jnp.int32)
    blocks = NBOX * CHORD_BLOCKS * NORMAL_BLOCKS

    def place(lattice, index):
        span_idx = (index // (CHORD_BLOCKS * NORMAL_BLOCKS)).astype(jnp.int32)
        chord_idx = ((index // NORMAL_BLOCKS) % CHORD_BLOCKS).astype(jnp.int32)
        normal_idx = (index % NORMAL_BLOCKS).astype(jnp.int32)
        block = lax.dynamic_slice(mesh_adjoint, (zero, span_idx * CX, chord_idx * CY, normal_idx * CZ), (3, CX, CY, CZ))
        window = ffd_window(block)
        box_id = box_map[span_idx, chord_idx, normal_idx].astype(jnp.int32)
        corner = offsets[span_idx, chord_idx, normal_idx].astype(jnp.int32)
        where = (box_id, zero, corner[0], corner[1], corner[2])
        current = lax.dynamic_slice(lattice, where, (1, 3, WA, WB, WC))
        return lax.dynamic_update_slice(lattice, current + window[None], where), None

    lattice = jnp.zeros((NBOX, 3, LA, LB, LC), jnp.float32)
    lattice, unused = lax.scan(place, lattice, jnp.arange(blocks, dtype=jnp.int32))
    return mesh_adjoint, lattice.reshape(NBOX, 3, LAT)
```

```python
import functools
import math

import jax
import jax.numpy as jnp
import numpy as np
from jax import lax
from jax.experimental import pallas as pl
from jax.experimental.pallas import tpu as pltpu
from jax.sharding import PartitionSpec as P

F32 = jnp.float32
HIGHEST = lax.Precision.HIGHEST
CN = ("chord", "normal")
CX, CY, CZ = 8, 8, 128
LA, LB, LC = 96, 32, 16
ROWS = LA // 16
SLOT = 32
KEEP = 24


def bernstein(count, cells):
    degree = count - 1
    u = (np.arange(cells) + 0.5) / cells
    return np.stack([math.comb(degree, a) * u**a * (1 - u) ** (degree - a) for a in range(count)])


def tables():
    bx, by, bz = bernstein(8, CX), bernstein(8, CY), bernstein(8, CZ)
    along_z = np.zeros((CZ, 8, 16))
    along_z[:, :, :8] = bz.T[:, None, :]
    along_y = np.repeat(by.T, 16, axis=1)
    along_x = np.zeros((3, 8, 3, CX, CY))
    for r in range(3):
        along_x[r, :, r] = 8.0 * bx[:, :, None]
    return (
        along_z.reshape(CZ, 128).astype(np.float32),
        along_y.astype(np.float32),
        along_x.reshape(24, 192).astype(np.float32),
    )


def iotas():
    lane = lax.broadcasted_iota(jnp.int32, (8, 128), 1)
    row = lax.broadcasted_iota(jnp.int32, (8, 128), 0)
    return lane, row


def places():
    c = lax.axis_index("chord")
    n = lax.axis_index("normal")
    before = (jnp.maximum(c - 1, 0) * 4 + n, c * 4 + jnp.maximum(n - 1, 0))
    after = (jnp.minimum(c + 1, 3) * 4 + n, c * 4 + jnp.minimum(n + 1, 3))
    return c, n, before, after


def pack(tile_of, fields, first_ref, last_ref, slots_ref):
    lane, _ = iotas()
    _, _, before, after = places()
    low = jnp.zeros((8, 128), F32)
    high = jnp.zeros((8, 128), F32)
    for v in range(fields):
        for x in range(CX):
            tile = tile_of(v, x)
            k = v * CX + x
            if x == 0:
                first_ref[v] = tile
            if x == CX - 1:
                last_ref[v] = tile
            slots_ref[before[0], k : k + 1, :] = tile[0:1, :]
            slots_ref[after[0], k : k + 1, :] = tile[7:8, :]
            low = jnp.where(lane == k, pltpu.roll(tile, k, 1) if k else tile, low)
            high = jnp.where(lane == k, pltpu.roll(tile, k + 1, 1), high)
    slots_ref[before[1], 0:8, :] = low
    slots_ref[after[1], 0:8, :] = high


def unpack(fields, slots_ref, rows_ref):
    c, n, before, after = places()
    count = fields * CX
    rows_ref[0] = jnp.where(c > 0, slots_ref[before[0], 0:count, :], 0.0)
    rows_ref[1] = jnp.where(c < 3, slots_ref[after[0], 0:count, :], 0.0)
    low = jnp.where(n > 0, slots_ref[before[1], 0:8, :], 0.0)
    high = jnp.where(n < 3, slots_ref[after[1], 0:8, :], 0.0)
    return low, high


def neighbours(tile_of, v, x, xlo_ref, xhi_ref, rows_ref, low, high):
    lane, row = iotas()
    k = v * CX + x
    tile = tile_of(v, x)
    west = xlo_ref[v] if x == 0 else tile_of(v, x - 1)
    east = xhi_ref[v] if x == CX - 1 else tile_of(v, x + 1)
    south = jnp.where(row == 0, rows_ref[0, k : k + 1, :], pltpu.roll(tile, 1, 0))
    north = jnp.where(row == 7, rows_ref[1, k : k + 1, :], pltpu.roll(tile, 7, 0))
    down = jnp.where(lane == 0, pltpu.roll(low, (128 - k) % 128, 1) if k else low, pltpu.roll(tile, 1, 1))
    up = jnp.where(lane == 127, pltpu.roll(high, 127 - k, 1), pltpu.roll(tile, 127, 1))
    return [tile, west, east, south, north, down, up]


def edges_kernel(adjoint_ref, first_ref, last_ref, slots_ref):
    pack(lambda v, x: adjoint_ref[v, x], 5, first_ref, last_ref, slots_ref)


def flux_kernel(
    wall_ref, map_ref, adjoint_ref, jacobian_ref, face_ref, stiff_ref, xlo_ref, xhi_ref, slots_ref,
    out_ref, first_ref, last_ref, send_ref, rows_ref,
):
    lane, row = iotas()
    n = lax.axis_index("normal")
    low, high = unpack(5, slots_ref, rows_ref)
    tile_of = lambda v, x: adjoint_ref[v, x]
    on_wall = (lane == 0) & (n == 0)
    for x in range(CX):
        total = [jnp.zeros((8, 128), F32) for _ in range(5)]
        faces = jnp.broadcast_to(face_ref[x : x + 1, :], (8, 8))
        square = lax.broadcasted_iota(jnp.int32, (8, 8), 0) == lax.broadcasted_iota(jnp.int32, (8, 8), 1)
        face = jnp.sum(jnp.where(square, faces.astype(F32), 0.0), axis=1, keepdims=True)
        kind = [on_wall & (jnp.broadcast_to(face, (8, 128)) == float(t)) for t in range(3)]
        for p in range(5):
            views = neighbours(tile_of, p, x, xlo_ref, xhi_ref, rows_ref, low, high)
            for e in range(7):
                for q in range(5):
                    total[q] = total[q] + jacobian_ref[e, p, q, x].astype(F32) * views[e]
            for t in range(3):
                part = jnp.where(kind[t], views[0], 0.0)
                for q in range(5):
                    total[q] = total[q] + wall_ref[t, p * 5 + q] * part
        diagonal = stiff_ref[0, x]
        for e in range(1, 7):
            diagonal = diagonal + stiff_ref[e, x]
        inverse = 1.0 / diagonal
        for r in range(3):
            sens = map_ref[r, 0] * total[0]
            for q in range(1, 5):
                sens = sens + map_ref[r, q] * total[q]
            out_ref[r, x] = sens * inverse
    pack(lambda v, x: out_ref[v, x], 3, first_ref, last_ref, send_ref)


def sweep(now_ref, start_ref, stiff_ref, xlo_ref, xhi_ref, slots_ref, rows_ref, store):
    low, high = unpack(3, slots_ref, rows_ref)
    tile_of = lambda v, x: now_ref[v, x]
    for x in range(CX):
        diagonal = stiff_ref[0, x]
        for e in range(1, 7):
            diagonal = diagonal + stiff_ref[e, x]
        inverse = 1.0 / diagonal
        for v in range(3):
            views = neighbours(tile_of, v, x, xlo_ref, xhi_ref, rows_ref, low, high)
            total = stiff_ref[1, x] * views[1]
            for e in range(2, 7):
                total = total + stiff_ref[e, x] * views[e]
            store(v, x, start_ref[v, x] + total * inverse)


def middle_kernel(
    start_ref, stiff_ref, xlo_ref, xhi_ref, slots_ref, out_ref, first_ref, last_ref, send_ref, rows_ref
):
    def store(v, x, tile):
        out_ref[v, x] = tile

    sweep(start_ref, start_ref, stiff_ref, xlo_ref, xhi_ref, slots_ref, rows_ref, store)
    pack(lambda v, x: out_ref[v, x], 3, first_ref, last_ref, send_ref)


def window_kernel(
    box_ref, corner_ref, now_ref, start_ref, stiff_ref, xlo_ref, xhi_ref, slots_ref,
    bz_ref, by_ref, bx_ref, out_ref, send_ref, rows_ref, flat_ref,
):
    def store(v, x, tile):
        out_ref[v, x] = tile
        base = (v * CX + x) * CY
        flat_ref[base : base + CY, :] = tile

    sweep(now_ref, start_ref, stiff_ref, xlo_ref, xhi_ref, slots_ref, rows_ref, store)
    inner = jnp.dot(flat_ref[...], bz_ref[...], precision=HIGHEST, preferred_element_type=F32)
    inner = inner * jnp.concatenate([by_ref[...]] * 24, axis=0)
    window = jnp.dot(bx_ref[...], inner, precision=HIGHEST, preferred_element_type=F32)
    lane, row = iotas()
    box = box_ref[0]
    oa, ob, oc = corner_ref[0], corner_ref[1], corner_ref[2]
    shift = oc + 16 * lax.rem(ob, 8)
    window = pltpu.roll(window, shift, 1)
    block = lax.div(ob, 8) + jnp.where(lane < shift, 1, 0)
    for s in range(16):
        where = jnp.where(box == s, block, -1)
        send_ref[s, 0:24, :] = window
        send_ref[s, 24:32, :] = jnp.where(row == 0, where, oa).astype(F32)


def place_kernel(got_ref, send_ref, wide_ref):
    lane, _ = iotas()
    target = jnp.zeros((8, 128), F32)
    for w in range(16):
        where = jnp.broadcast_to(got_ref[w, 24:25, :], (8, 128))
        start = jnp.broadcast_to(got_ref[w, 25:26, :], (8, 128))
        target = jnp.where(lane // 8 == w, start, target)
        for r in range(3):
            tile = got_ref[w, r * 8 : r * 8 + 8, :]
            for block in range(4):
                wide_ref[r, w * 8 : w * 8 + 8, block * 128 : block * 128 + 128] = jnp.where(
                    where == float(block), tile, 0.0
                )
    target = target + lax.rem(lane, 8).astype(F32)
    line = lax.broadcasted_iota(jnp.int32, (128, 128), 0)
    point = (line // 8) * ROWS + lax.rem(line, 8)
    point = jnp.where(lax.rem(line, 8) < ROWS, point, -1).astype(F32)
    pick = jnp.where(point == jnp.concatenate([target] * 16, axis=0), 1.0, 0.0).astype(F32)
    for r in range(3):
        placed = jnp.dot(pick, wide_ref[r], precision=HIGHEST, preferred_element_type=F32)
        for j in range(16):
            for block in range(4):
                base = (r * 4 + block) * ROWS
                send_ref[j, base : base + ROWS, :] = placed[
                    j * 8 : j * 8 + ROWS, block * 128 : block * 128 + 128
                ]


def sum_kernel(got_ref, out_ref, total_ref):
    total = got_ref[0]
    for j in range(1, 16):
        total = total + got_ref[j]
    total_ref[...] = total
    for r in range(3):
        for block in range(4):
            for a in range(ROWS):
                base = a * 512 + block * 128
                at = (r * 4 + block) * ROWS + a
                out_ref[0, r : r + 1, base : base + 128] = total_ref[at : at + 1, :]


VMEM = pl.BlockSpec(memory_space=pltpu.VMEM)
SMEM = pl.BlockSpec(memory_space=pltpu.SMEM)


def shape(*dims):
    return jax.ShapeDtypeStruct(dims, F32)


def call(body, outs, ins, scratch=(), scalars=0, limit=24, name=None):
    return pl.pallas_call(
        body,
        out_shape=outs,
        in_specs=[SMEM] * scalars + [VMEM] * (len(ins) - scalars),
        out_specs=jax.tree.map(lambda _: VMEM, outs),
        scratch_shapes=[pltpu.VMEM(dims, F32) for dims in scratch],
        compiler_params=pltpu.CompilerParams(vmem_limit_bytes=limit << 20),
        name=name,
    )(*ins)


def swap(first, last, slots):
    count = lax.axis_size("span")
    up = [(i, i + 1) for i in range(count - 1)]
    down = [(j, i) for i, j in up]
    got = lax.all_to_all(slots, CN, 0, 0, tiled=True)
    before = lax.ppermute(last, "span", up)
    after = lax.ppermute(first, "span", down)
    return before, after, got


def local(adjoint, jacobian, wall_table, face_type, mesh_map, stiffness, box_map, offsets):
    ends = lambda v, rows: (shape(v, 8, 128), shape(v, 8, 128), shape(16, rows, 128))
    block = shape(3, CX, CY, CZ)
    halo = swap(*call(edges_kernel, ends(5, 40), (adjoint,), name="edges"))
    start, *out = call(
        flux_kernel,
        (block, *ends(3, KEEP)),
        (wall_table.reshape(3, 25), mesh_map, adjoint, jacobian, face_type, stiffness, *halo),
        scratch=((2, 40, 128),),
        scalars=2,
        name="flux",
    )
    halo = swap(*out)
    middle, *out = call(
        middle_kernel, (block, *ends(3, KEEP)), (start, stiffness, *halo), scratch=((2, 24, 128),), name="middle"
    )
    halo = swap(*out)
    bz, by, bx = tables()
    final, windows = call(
        window_kernel,
        (block, shape(16, SLOT, 128)),
        (box_map.reshape(1), offsets.reshape(3), middle, start, stiffness, *halo, bz, by, bx),
        scratch=((2, 24, 128), (192, 128)),
        scalars=2,
        name="window",
    )
    got = lax.all_to_all(windows, "span", 0, 0, tiled=True)
    chunks = call(place_kernel, shape(16, 72, 128), (got,), scratch=((3, 128, 512),), name="place")
    got = lax.all_to_all(chunks, CN, 0, 0, tiled=True)
    grad = call(sum_kernel, shape(1, 3, 3072), (got,), scratch=((72, 128),), name="sums")
    return final, grad


def solution(mesh):
    placed = (
        P(None, "span", "chord", "normal"),
        P(None, None, None, "span", "chord", "normal"),
        P(),
        P("span", "chord"),
        P(),
        P(None, "span", "chord", "normal"),
        P("span", "chord", "normal"),
        P("span", "chord", "normal", None),
    )
    return jax.shard_map(
        local,
        mesh=mesh,
        in_specs=placed,
        out_specs=(P(None, "span", "chord", "normal"), P("span", None, ("chord", "normal"))),
        check_vma=False,
    )
```

```python
import functools
import math

import jax
import jax.numpy as jnp
import numpy as np
from jax import lax
from jax.experimental import pallas as pl
from jax.experimental.pallas import tpu as pltpu
from jax.sharding import PartitionSpec as P

F32 = jnp.float32
HIGHEST = lax.Precision.HIGHEST
CN = ("chord", "normal")
CX, CY, CZ = 8, 8, 128
LA, LB, LC = 96, 32, 16
ROWS = LA // 16
SLOT = 32


def bernstein(count, cells):
    degree = count - 1
    u = (np.arange(cells) + 0.5) / cells
    return np.stack([math.comb(degree, a) * u**a * (1 - u) ** (degree - a) for a in range(count)])


def tables():
    bx, by, bz = bernstein(8, CX), bernstein(8, CY), bernstein(8, CZ)
    along_z = np.zeros((CZ, 8, 16))
    along_z[:, :, :8] = bz.T[:, None, :]
    along_y = np.repeat(by.T, 16, axis=1)
    along_x = np.zeros((3, 8, 3, CX, CY))
    for r in range(3):
        along_x[r, :, r] = 8.0 * bx[:, :, None]
    return (
        along_z.reshape(CZ, 128).astype(np.float32),
        along_y.astype(np.float32),
        along_x.reshape(24, 192).astype(np.float32),
    )


def iotas():
    lane = lax.broadcasted_iota(jnp.int32, (8, 128), 1)
    row = lax.broadcasted_iota(jnp.int32, (8, 128), 0)
    return lane, row


def odd(axis):
    return lax.rem(lax.axis_index(axis), 2) == 1


def pick(flag, one, two):
    return jnp.where(jnp.full(one.shape, flag), one, two)


def pack(tile_of, fields, sends):
    lane, _ = iotas()
    xa, xb, ya, yb, za, zb = sends
    by_x, by_y, by_z = odd("span"), odd("chord"), odd("normal")
    low = jnp.zeros((8, 128), F32)
    high = jnp.zeros((8, 128), F32)
    for v in range(fields):
        first, last = tile_of(v, 0), tile_of(v, CX - 1)
        xa[v] = pick(by_x, first, last)
        xb[v] = pick(by_x, last, first)
        for x in range(CX):
            tile = tile_of(v, x)
            k = v * CX + x
            ya[k : k + 1, :] = pick(by_y, tile[0:1, :], tile[7:8, :])
            yb[k : k + 1, :] = pick(by_y, tile[7:8, :], tile[0:1, :])
            low = jnp.where(lane == k, pltpu.roll(tile, k, 1) if k else tile, low)
            high = jnp.where(lane == k, pltpu.roll(tile, k + 1, 1), high)
    za[...] = pick(by_z, low, high)
    zb[...] = pick(by_z, high, low)


def unpack(halo, planes_ref, rows_ref):
    xa, xb, ya, yb, za, zb = halo
    by_x, by_y, by_z = odd("span"), odd("chord"), odd("normal")
    planes_ref[0] = pick(by_x, xa[...], xb[...])
    planes_ref[1] = pick(by_x, xb[...], xa[...])
    rows_ref[0] = pick(by_y, ya[...], yb[...])
    rows_ref[1] = pick(by_y, yb[...], ya[...])
    return pick(by_z, za[...], zb[...]), pick(by_z, zb[...], za[...])


def neighbour(e, tile_of, v, x, planes_ref, rows_ref, low, high):
    lane, row = iotas()
    k = v * CX + x
    if e == 1:
        return planes_ref[0, v] if x == 0 else tile_of(v, x - 1)
    if e == 2:
        return planes_ref[1, v] if x == CX - 1 else tile_of(v, x + 1)
    tile = tile_of(v, x)
    if e == 0:
        return tile
    if e == 3:
        return jnp.where(row == 0, rows_ref[0, k : k + 1, :], pltpu.roll(tile, 1, 0))
    if e == 4:
        return jnp.where(row == 7, rows_ref[1, k : k + 1, :], pltpu.roll(tile, 7, 0))
    if e == 5:
        return jnp.where(lane == 0, pltpu.roll(low, (128 - k) % 128, 1) if k else low, pltpu.roll(tile, 1, 1))
    return jnp.where(lane == 127, pltpu.roll(high, 127 - k, 1), pltpu.roll(tile, 127, 1))


def edges_kernel(adjoint_any, *refs):
    sends, (adjoint_ref, sem) = refs[:6], refs[6:]
    fetch = pltpu.make_async_copy(adjoint_any, adjoint_ref, sem)
    fetch.start()
    fetch.wait()
    pack(lambda v, x: adjoint_ref[v, x], 5, sends)


def flux_kernel(wall_any, map_any, adjoint_any, jacobian_any, face_any, stiff_any, *refs):
    halo, out_ref, sends = refs[:6], refs[6], refs[7:13]
    wall_ref, map_ref, adjoint_ref, jacobian_ref, face_ref, stiff_ref, total_ref, planes_ref, rows_ref, sems = refs[13:]
    copies = [
        pltpu.make_async_copy(wall_any, wall_ref, sems.at[0]),
        pltpu.make_async_copy(map_any, map_ref, sems.at[1]),
        pltpu.make_async_copy(adjoint_any, adjoint_ref, sems.at[2]),
        pltpu.make_async_copy(face_any, face_ref, sems.at[3]),
        pltpu.make_async_copy(stiff_any, stiff_ref, sems.at[4]),
    ]
    parts = [pltpu.make_async_copy(jacobian_any.at[e], jacobian_ref.at[e], sems.at[5 + e]) for e in range(7)]
    for copy in (copies[2], *parts, *copies[:2], copies[3], copies[4]):
        copy.start()
    lane, row = iotas()
    on_wall = (lane == 0) & (lax.axis_index("normal") == 0)
    low, high = unpack(halo, planes_ref, rows_ref)
    tile_of = lambda v, x: adjoint_ref[v, x]
    copies[2].wait()
    for e in range(7):
        parts[e].wait()
        for x in range(CX):
            views = [neighbour(e, tile_of, p, x, planes_ref, rows_ref, low, high) for p in range(5)]
            total = [jnp.zeros((8, 128), F32) if e == 0 else total_ref[q, x] for q in range(5)]
            for p in range(5):
                for q in range(5):
                    total[q] = total[q] + jacobian_ref[e, p, q, x].astype(F32) * views[p]
            for q in range(5):
                total_ref[q, x] = total[q]
    for copy in (*copies[:2], *copies[3:]):
        copy.wait()
    square = lax.broadcasted_iota(jnp.int32, (8, 8), 0) == lax.broadcasted_iota(jnp.int32, (8, 8), 1)
    for x in range(CX):
        total = [total_ref[q, x] for q in range(5)]
        faces = jnp.broadcast_to(face_ref[x : x + 1, :], (8, 8)).astype(F32)
        face = jnp.sum(jnp.where(square, faces, 0.0), axis=1, keepdims=True)
        face = jnp.broadcast_to(face, (8, 128))
        for t in range(3):
            mask = on_wall & (face == float(t))
            for p in range(5):
                part = jnp.where(mask, adjoint_ref[p, x], 0.0)
                for q in range(5):
                    total[q] = total[q] + wall_ref[p, t, q] * part
        inverse = inverse_diagonal(stiff_ref, x)
        for r in range(3):
            sens = map_ref[r, 0] * total[0]
            for q in range(1, 5):
                sens = sens + map_ref[r, q] * total[q]
            out_ref[r, x] = sens * inverse
    pack(lambda v, x: out_ref[v, x], 3, sends)


def inverse_diagonal(stiff_ref, x):
    diagonal = stiff_ref[0, x]
    for e in range(1, 7):
        diagonal = diagonal + stiff_ref[e, x]
    return 1.0 / diagonal


def sweep(now_ref, start_ref, stiff_ref, halo, planes_ref, rows_ref, store):
    low, high = unpack(halo, planes_ref, rows_ref)
    tile_of = lambda v, x: now_ref[v, x]
    for x in range(CX):
        inverse = inverse_diagonal(stiff_ref, x)
        for v in range(3):
            total = stiff_ref[1, x] * neighbour(1, tile_of, v, x, planes_ref, rows_ref, low, high)
            for e in range(2, 7):
                total = total + stiff_ref[e, x] * neighbour(e, tile_of, v, x, planes_ref, rows_ref, low, high)
            store(v, x, start_ref[v, x] + total * inverse)


def middle_kernel(start_ref, stiff_ref, *refs):
    halo, out_ref, sends, planes_ref, rows_ref = refs[:6], refs[6], refs[7:13], *refs[13:]

    def store(v, x, tile):
        out_ref[v, x] = tile

    sweep(start_ref, start_ref, stiff_ref, halo, planes_ref, rows_ref, store)
    pack(lambda v, x: out_ref[v, x], 3, sends)


def window_kernel(box_ref, corner_ref, now_ref, start_ref, stiff_ref, bz_ref, by_ref, bx_ref, *refs):
    halo, out_ref, send_ref, planes_ref, rows_ref, flat_ref = refs[:6], *refs[6:]

    def store(v, x, tile):
        out_ref[v, x] = tile
        base = (v * CX + x) * CY
        flat_ref[base : base + CY, :] = tile

    sweep(now_ref, start_ref, stiff_ref, halo, planes_ref, rows_ref, store)
    inner = jnp.dot(flat_ref[...], bz_ref[...], precision=HIGHEST, preferred_element_type=F32)
    inner = inner * jnp.concatenate([by_ref[...]] * 24, axis=0)
    window = jnp.dot(bx_ref[...], inner, precision=HIGHEST, preferred_element_type=F32)
    lane, row = iotas()
    box = box_ref[0]
    oa, ob, oc = corner_ref[0], corner_ref[1], corner_ref[2]
    shift = oc + 16 * lax.rem(ob, 8)
    window = pltpu.roll(window, shift, 1)
    block = lax.div(ob, 8) + jnp.where(lane < shift, 1, 0)
    for s in range(16):
        where = jnp.where(box == s, block, -1)
        send_ref[s, 0:24, :] = window
        send_ref[s, 24:32, :] = jnp.where(row == 0, where, oa).astype(F32)


def place_kernel(got_ref, send_ref, wide_ref):
    lane, _ = iotas()
    target = jnp.zeros((8, 128), F32)
    for w in range(16):
        where = jnp.broadcast_to(got_ref[w, 24:25, :], (8, 128))
        start = jnp.broadcast_to(got_ref[w, 25:26, :], (8, 128))
        target = jnp.where(lane // 8 == w, start, target)
        for r in range(3):
            tile = got_ref[w, r * 8 : r * 8 + 8, :]
            for block in range(4):
                wide_ref[r, w * 8 : w * 8 + 8, block * 128 : block * 128 + 128] = jnp.where(
                    where == float(block), tile, 0.0
                )
    target = target + lax.rem(lane, 8).astype(F32)
    line = lax.broadcasted_iota(jnp.int32, (128, 128), 0)
    point = (line // 8) * ROWS + lax.rem(line, 8)
    point = jnp.where(lax.rem(line, 8) < ROWS, point, -1).astype(F32)
    hits = jnp.where(point == jnp.concatenate([target] * 16, axis=0), 1.0, 0.0).astype(F32)
    for r in range(3):
        placed = jnp.dot(hits, wide_ref[r], precision=HIGHEST, preferred_element_type=F32)
        for j in range(16):
            for block in range(4):
                base = (r * 4 + block) * ROWS
                send_ref[j, base : base + ROWS, :] = placed[
                    j * 8 : j * 8 + ROWS, block * 128 : block * 128 + 128
                ]


def sum_kernel(got_ref, out_ref, total_ref):
    total = got_ref[0]
    for j in range(1, 16):
        total = total + got_ref[j]
    total_ref[...] = total
    for r in range(3):
        for block in range(4):
            for a in range(ROWS):
                base = a * 512 + block * 128
                at = (r * 4 + block) * ROWS + a
                out_ref[r, 0:1, base : base + 128] = total_ref[at : at + 1, :]


VMEM = pl.BlockSpec(memory_space=pltpu.VMEM)
SMEM = pl.BlockSpec(memory_space=pltpu.SMEM)


def shape(*dims):
    return jax.ShapeDtypeStruct(dims, F32)


def call(body, outs, ins, scratch=(), scalars=0, limit=24 << 20, name=None, remote=()):
    specs = [SMEM] * scalars + [VMEM] * (len(ins) - scalars)
    for at in remote:
        specs[at] = HBM
    return pl.pallas_call(
        body,
        out_shape=outs,
        in_specs=specs,
        out_specs=jax.tree.map(lambda _: VMEM, outs),
        scratch_shapes=[pltpu.VMEM(a, F32) if isinstance(a, tuple) else a for a in scratch],
        compiler_params=pltpu.CompilerParams(vmem_limit_bytes=limit),
        name=name,
    )(*ins)


def in_hbm(one):
    return pltpu.with_memory_space_constraint(one, pltpu.HBM)


HBM = pl.BlockSpec(memory_space=pltpu.HBM)
DMA = pltpu.SemaphoreType.DMA


def pairings(axis):
    count = lax.axis_size(axis)
    for start in (0, 1):
        pairs = [(i, i + 1) for i in range(start, count - 1, 2)]
        yield pairs + [(j, i) for i, j in pairs]


def swap(*sends):
    got = []
    for axis, pair in zip(("span", "chord", "normal"), (sends[0:2], sends[2:4], sends[4:6])):
        got += [lax.ppermute(one, axis, pairs) for one, pairs in zip(pair, pairings(axis))]
    return got


def ends(v):
    return (shape(v, 8, 128),) * 2 + (shape(v * 8, 128),) * 2 + (shape(8, 128),) * 2


def local(adjoint, jacobian, wall_table, face_type, mesh_map, stiffness, box_map, offsets):
    block = shape(3, CX, CY, CZ)
    out = call(
        edges_kernel,
        ends(5),
        (in_hbm(adjoint),),
        scratch=((5, CX, CY, CZ), DMA),
        remote=(0,),
        name="edges",
    )
    halo = swap(*out)
    fixed = (wall_table.transpose(1, 0, 2), mesh_map, adjoint, jacobian, face_type, stiffness)
    spaces = (pltpu.SMEM, pltpu.SMEM) + (pltpu.VMEM,) * 4
    start, *out = call(
        flux_kernel,
        (block, *ends(3)),
        (*map(in_hbm, fixed), *halo),
        scratch=(
            *(space(one.shape, one.dtype) for space, one in zip(spaces, fixed)),
            (5, CX, CY, CZ),
            (2, 5, 8, 128),
            (2, 40, 128),
            DMA((12,)),
        ),
        remote=range(6),
        name="flux",
    )
    halo = swap(*out)
    kept = ((2, 3, 8, 128), (2, 24, 128))
    middle, *out = call(middle_kernel, (block, *ends(3)), (start, stiffness, *halo), scratch=kept, name="middle")
    halo = swap(*out)
    bz, by, bx = tables()
    final, windows = call(
        window_kernel,
        (block, shape(16, SLOT, 128)),
        (box_map.reshape(1), offsets.reshape(3), middle, start, stiffness, bz, by, bx, *halo),
        scratch=(*kept, (192, 128)),
        scalars=2,
        name="window",
    )
    got = lax.all_to_all(windows, "span", 0, 0, tiled=True)
    chunks = call(place_kernel, shape(16, 72, 128), (got,), scratch=((3, 128, 512),), name="place")
    got = lax.all_to_all(chunks, CN, 0, 0, tiled=True)
    grad = call(sum_kernel, shape(3, 1, 3072), (got,), scratch=((72, 128),), name="sums")
    return final, grad.reshape(1, 3, 3072)


def solution(mesh):
    placed = (
        P(None, "span", "chord", "normal"),
        P(None, None, None, "span", "chord", "normal"),
        P(),
        P("span", "chord"),
        P(),
        P(None, "span", "chord", "normal"),
        P("span", "chord", "normal"),
        P("span", "chord", "normal", None),
    )
    return jax.shard_map(
        local,
        mesh=mesh,
        in_specs=placed,
        out_specs=(P(None, "span", "chord", "normal"), P("span", None, ("chord", "normal"))),
        check_vma=False,
    )
```

```python
import math

import jax
import jax.numpy as jnp
import numpy as np
from jax import lax
from jax.experimental import pallas as pl
from jax.experimental.pallas import tpu as pltpu
from jax.sharding import PartitionSpec as P

F32 = jnp.float32
HIGHEST = lax.Precision.HIGHEST
ALL = ("span", "chord", "normal")
CX, CY, CZ = 8, 8, 128
LA = 96
ROWS = LA // 16
SLOT = 16
WINDOWS = 32


def bernstein(count, cells):
    degree = count - 1
    u = (np.arange(cells) + 0.5) / cells
    return np.stack([math.comb(degree, a) * u**a * (1 - u) ** (degree - a) for a in range(count)])


def tables():
    bx, by, bz = bernstein(8, CX), bernstein(8, CY), bernstein(8, CZ)
    along_z = np.zeros((CZ, 8, 2, 8))
    along_z[:] = bz.T[:, None, None, :]
    along_y = np.repeat(by.T, 16, axis=1)
    along_x = np.zeros((2, 4, 4, 3, CX, CY))
    for r in range(3):
        along_x[:, r, :, r] = 8.0 * bx.reshape(2, 4, CX)[..., None]
    return (
        along_z.reshape(CZ, 128).astype(np.float32),
        along_y.astype(np.float32),
        along_x.reshape(32, 192).astype(np.float32),
    )


def iotas():
    lane = lax.broadcasted_iota(jnp.int32, (8, 128), 1)
    row = lax.broadcasted_iota(jnp.int32, (8, 128), 0)
    return lane, row


def odd(axis):
    return lax.rem(lax.axis_index(axis), 2) == 1


def pick(flag, one, two):
    return jnp.where(jnp.full(one.shape, flag), one, two)


def pack(tile_of, fields, sends):
    lane, _ = iotas()
    xa, xb, ya, yb, za, zb = sends
    by_x, by_y, by_z = odd("span"), odd("chord"), odd("normal")
    low = jnp.zeros((8, 128), F32)
    high = jnp.zeros((8, 128), F32)
    for v in range(fields):
        first, last = tile_of(v, 0), tile_of(v, CX - 1)
        xa[v] = pick(by_x, first, last)
        xb[v] = pick(by_x, last, first)
        for x in range(CX):
            tile = tile_of(v, x)
            k = v * CX + x
            ya[k : k + 1, :] = pick(by_y, tile[0:1, :], tile[7:8, :])
            yb[k : k + 1, :] = pick(by_y, tile[7:8, :], tile[0:1, :])
            low = jnp.where(lane == k, pltpu.roll(tile, k, 1) if k else tile, low)
            high = jnp.where(lane == k, pltpu.roll(tile, k + 1, 1), high)
    za[...] = pick(by_z, low, high)
    zb[...] = pick(by_z, high, low)


def unpack(halo, planes_ref, rows_ref):
    xa, xb, ya, yb, za, zb = halo
    by_x, by_y, by_z = odd("span"), odd("chord"), odd("normal")
    planes_ref[0] = pick(by_x, xa[...], xb[...])
    planes_ref[1] = pick(by_x, xb[...], xa[...])
    rows_ref[0] = pick(by_y, ya[...], yb[...])
    rows_ref[1] = pick(by_y, yb[...], ya[...])
    return pick(by_z, za[...], zb[...]), pick(by_z, zb[...], za[...])


def neighbour(e, tile_of, v, x, planes_ref, rows_ref, low, high):
    lane, row = iotas()
    k = v * CX + x
    if e == 1:
        return planes_ref[0, v] if x == 0 else tile_of(v, x - 1)
    if e == 2:
        return planes_ref[1, v] if x == CX - 1 else tile_of(v, x + 1)
    tile = tile_of(v, x)
    if e == 0:
        return tile
    if e == 3:
        return jnp.where(row == 0, rows_ref[0, k : k + 1, :], pltpu.roll(tile, 1, 0))
    if e == 4:
        return jnp.where(row == 7, rows_ref[1, k : k + 1, :], pltpu.roll(tile, 7, 0))
    if e == 5:
        return jnp.where(lane == 0, pltpu.roll(low, (128 - k) % 128, 1) if k else low, pltpu.roll(tile, 1, 1))
    return jnp.where(lane == 127, pltpu.roll(high, 127 - k, 1), pltpu.roll(tile, 127, 1))


def edges_kernel(adjoint_any, *refs):
    sends, (adjoint_ref, sem) = refs[:6], refs[6:]
    fetch = pltpu.make_async_copy(adjoint_any, adjoint_ref, sem)
    fetch.start()
    fetch.wait()
    pack(lambda v, x: adjoint_ref[v, x], 5, sends)


def flux_kernel(wall_any, map_any, adjoint_any, jacobian_any, face_any, stiff_any, *refs):
    halo, out_ref, sends = refs[:6], refs[6], refs[7:13]
    wall_ref, map_ref, adjoint_ref, jacobian_ref, face_ref, stiff_ref, total_ref, planes_ref, rows_ref, sems = refs[13:]
    copies = [
        pltpu.make_async_copy(wall_any, wall_ref, sems.at[0]),
        pltpu.make_async_copy(map_any, map_ref, sems.at[1]),
        pltpu.make_async_copy(adjoint_any, adjoint_ref, sems.at[2]),
        pltpu.make_async_copy(face_any, face_ref, sems.at[3]),
        pltpu.make_async_copy(stiff_any, stiff_ref, sems.at[4]),
    ]
    parts = [pltpu.make_async_copy(jacobian_any.at[e], jacobian_ref.at[e], sems.at[5 + e]) for e in range(7)]
    for copy in (copies[2], *parts, *copies[:2], copies[3], copies[4]):
        copy.start()
    lane, _ = iotas()
    on_wall = (lane == 0) & (lax.axis_index("normal") == 0)
    low, high = unpack(halo, planes_ref, rows_ref)
    tile_of = lambda v, x: adjoint_ref[v, x]
    copies[2].wait()
    for e in range(7):
        parts[e].wait()
        for x in range(CX):
            views = [neighbour(e, tile_of, p, x, planes_ref, rows_ref, low, high) for p in range(5)]
            total = [jnp.zeros((8, 128), F32) if e == 0 else total_ref[q, x] for q in range(5)]
            for p in range(5):
                for q in range(5):
                    total[q] = total[q] + jacobian_ref[e, p, q, x].astype(F32) * views[p]
            for q in range(5):
                total_ref[q, x] = total[q]
    for copy in (*copies[:2], *copies[3:]):
        copy.wait()
    square = lax.broadcasted_iota(jnp.int32, (8, 8), 0) == lax.broadcasted_iota(jnp.int32, (8, 8), 1)
    for x in range(CX):
        total = [total_ref[q, x] for q in range(5)]
        faces = jnp.broadcast_to(face_ref[x : x + 1, :], (8, 8)).astype(F32)
        face = jnp.sum(jnp.where(square, faces, 0.0), axis=1, keepdims=True)
        face = jnp.broadcast_to(face, (8, 128))
        for t in range(3):
            mask = on_wall & (face == float(t))
            for p in range(5):
                part = jnp.where(mask, adjoint_ref[p, x], 0.0)
                for q in range(5):
                    total[q] = total[q] + wall_ref[p, t, q] * part
        inverse = inverse_diagonal(stiff_ref, x)
        for r in range(3):
            sens = map_ref[r, 0] * total[0]
            for q in range(1, 5):
                sens = sens + map_ref[r, q] * total[q]
            out_ref[r, x] = sens * inverse
    pack(lambda v, x: out_ref[v, x], 3, sends)


def inverse_diagonal(stiff_ref, x):
    diagonal = stiff_ref[0, x]
    for e in range(1, 7):
        diagonal = diagonal + stiff_ref[e, x]
    return 1.0 / diagonal


def sweep(now_ref, start_ref, stiff_ref, halo, planes_ref, rows_ref, store):
    low, high = unpack(halo, planes_ref, rows_ref)
    tile_of = lambda v, x: now_ref[v, x]
    for x in range(CX):
        inverse = inverse_diagonal(stiff_ref, x)
        for v in range(3):
            total = stiff_ref[1, x] * neighbour(1, tile_of, v, x, planes_ref, rows_ref, low, high)
            for e in range(2, 7):
                total = total + stiff_ref[e, x] * neighbour(e, tile_of, v, x, planes_ref, rows_ref, low, high)
            store(v, x, start_ref[v, x] + total * inverse)


def middle_kernel(start_ref, stiff_ref, *refs):
    halo, out_ref, sends, planes_ref, rows_ref = refs[:6], refs[6], refs[7:13], *refs[13:]

    def store(v, x, tile):
        out_ref[v, x] = tile

    sweep(start_ref, start_ref, stiff_ref, halo, planes_ref, rows_ref, store)
    pack(lambda v, x: out_ref[v, x], 3, sends)


def window_kernel(box_ref, corner_ref, now_ref, start_ref, stiff_ref, bz_ref, by_ref, bx_ref, *refs):
    halo, out_ref, send_ref, planes_ref, rows_ref, flat_ref = refs[:6], *refs[6:]

    def store(v, x, tile):
        out_ref[v, x] = tile
        base = (v * CX + x) * CY
        flat_ref[base : base + CY, :] = tile

    sweep(now_ref, start_ref, stiff_ref, halo, planes_ref, rows_ref, store)
    inner = jnp.dot(flat_ref[...], bz_ref[...], precision=HIGHEST, preferred_element_type=F32)
    inner = inner * jnp.concatenate([by_ref[...]] * 24, axis=0)
    window = jnp.dot(bx_ref[...], inner, precision=HIGHEST, preferred_element_type=F32)
    lane = lax.broadcasted_iota(jnp.int32, (SLOT, 128), 1)
    row = lax.broadcasted_iota(jnp.int32, (SLOT, 128), 0)
    box = box_ref[0]
    oa, ob, oc = corner_ref[0], corner_ref[1], corner_ref[2]
    window = jnp.where(lax.rem(lane, 16) < 8, window[0:SLOT], window[SLOT : 2 * SLOT])
    shift = oc + 16 * lax.rem(ob, 8)
    window = pltpu.roll(window, shift, 1)
    inside = lax.rem(lane - shift + 128, 16) < 8
    block = jnp.where(inside, lax.div(ob, 8) + jnp.where(lane < shift, 1, 0), -1)
    for s in range(16):
        where = jnp.where(box == s, block, -1)
        there = jnp.where(row == 12, where, oa).astype(F32)
        there = jnp.where(row < 12, window, there)
        send_ref[2 * s] = there
        send_ref[2 * s + 1] = there


def place_kernel(got_ref, send_ref, wide_ref):
    half = lax.div(lax.axis_index("normal"), 2)
    where = got_ref[pl.ds(12, WINDOWS, stride=SLOT), :]
    start = got_ref[pl.ds(13, WINDOWS, stride=SLOT), :]
    lane = lax.broadcasted_iota(jnp.int32, (WINDOWS, 128), 1)
    row = lax.broadcasted_iota(jnp.int32, (WINDOWS, 128), 0)
    start = jnp.sum(jnp.where(lax.rem(lane, WINDOWS) == row, start, 0.0), axis=0, keepdims=True)
    step = lax.div(lax.broadcasted_iota(jnp.int32, (1, 128), 1), WINDOWS).astype(F32)
    first = start + step
    line = lax.broadcasted_iota(jnp.int32, (64, 128), 0)
    chunk = lax.div(line, 8)
    owner = lax.div(chunk, 2) * 4 + half * 2 + lax.rem(chunk, 2)
    point = jnp.where(lax.rem(line, 8) < ROWS, owner * ROWS + lax.rem(line, 8), -1).astype(F32)
    hits = jnp.concatenate(
        [jnp.where(point == jnp.broadcast_to(first + 4.0 * h, (64, 128)), 1.0, 0.0) for h in range(2)], axis=1
    )
    masks = [where == float(block) for block in range(4)]
    for r in range(3):
        for a in range(4):
            tile = got_ref[pl.ds(r * 4 + a, WINDOWS, stride=SLOT), :]
            for h in range(2):
                base = (h * 4 + a) * WINDOWS
                view = pltpu.roll(tile, 120, 1) if h else tile
                for block in range(4):
                    wide_ref[r, base : base + WINDOWS, block * 128 : block * 128 + 128] = jnp.where(
                        masks[block], view, 0.0
                    )
        placed = jnp.dot(hits, wide_ref[r], precision=HIGHEST, preferred_element_type=F32)
        for i in range(8):
            for block in range(4):
                base = (r * 4 + block) * ROWS
                send_ref[i, base : base + ROWS, :] = placed[
                    i * 8 : i * 8 + ROWS, block * 128 : block * 128 + 128
                ]


def sum_kernel(got_ref, out_ref, total_ref):
    total = got_ref[0]
    for j in range(1, 8):
        total = total + got_ref[j]
    total_ref[...] = total
    for r in range(3):
        for block in range(4):
            for a in range(ROWS):
                base = a * 512 + block * 128
                at = (r * 4 + block) * ROWS + a
                out_ref[r, 0:1, base : base + 128] = total_ref[at : at + 1, :]


VMEM = pl.BlockSpec(memory_space=pltpu.VMEM)
SMEM = pl.BlockSpec(memory_space=pltpu.SMEM)


def shape(*dims):
    return jax.ShapeDtypeStruct(dims, F32)


def call(body, outs, ins, scratch=(), scalars=0, limit=24 << 20, remote=()):
    specs = [SMEM] * scalars + [VMEM] * (len(ins) - scalars)
    for at in remote:
        specs[at] = HBM
    return pl.pallas_call(
        body,
        out_shape=outs,
        in_specs=specs,
        out_specs=jax.tree.map(lambda _: VMEM, outs),
        scratch_shapes=[pltpu.VMEM(a, F32) if isinstance(a, tuple) else a for a in scratch],
        compiler_params=pltpu.CompilerParams(vmem_limit_bytes=limit),
    )(*ins)


def in_hbm(one):
    return pltpu.with_memory_space_constraint(one, pltpu.HBM)


HBM = pl.BlockSpec(memory_space=pltpu.HBM)
DMA = pltpu.SemaphoreType.DMA


AXES = {"s": "span", "c": "chord", "n": "normal"}


def pairing(axis, start):
    pairs = [(i, i + 1) for i in range(start, lax.axis_size(axis) - 1, 2)]
    return pairs + [(j, i) for i, j in pairs]


def swap(*sends):
    got = []
    for at, one in enumerate(sends):
        name = "scn"[at // 2]
        got.append(lax.ppermute(one, AXES[name], pairing(AXES[name], at % 2)))
    return got


def ffd_groups():
    index = np.arange(256).reshape(16, 4, 2, 2)
    owners = index.transpose(1, 3, 0, 2).reshape(8, 32).tolist()
    sharers = index.transpose(0, 2, 1, 3).reshape(32, 8).tolist()
    return owners, sharers


def ends(v):
    return (shape(v, 8, 128),) * 2 + (shape(v * 8, 128),) * 2 + (shape(8, 128),) * 2


def local(adjoint, jacobian, wall_table, face_type, mesh_map, stiffness, box_map, offsets):
    block = shape(3, CX, CY, CZ)
    out = call(edges_kernel, ends(5), (in_hbm(adjoint),), scratch=((5, CX, CY, CZ), DMA), remote=(0,))
    halo = swap(*out)
    fixed = (wall_table.transpose(1, 0, 2), mesh_map, adjoint, jacobian, face_type, stiffness)
    spaces = (pltpu.SMEM, pltpu.SMEM) + (pltpu.VMEM,) * 4
    start, *out = call(
        flux_kernel,
        (block, *ends(3)),
        (*map(in_hbm, fixed), *halo),
        scratch=(
            *(space(one.shape, one.dtype) for space, one in zip(spaces, fixed)),
            (5, CX, CY, CZ),
            (2, 5, 8, 128),
            (2, 40, 128),
            DMA((12,)),
        ),
        remote=range(6),
    )
    halo = swap(*out)
    kept = ((2, 3, 8, 128), (2, 24, 128))
    middle, *out = call(middle_kernel, (block, *ends(3)), (start, stiffness, *halo), scratch=kept)
    halo = swap(*out)
    bz, by, bx = tables()
    final, windows = call(
        window_kernel,
        (block, shape(WINDOWS, SLOT, 128)),
        (box_map.reshape(1), offsets.reshape(3), middle, start, stiffness, bz, by, bx, *halo),
        scratch=(*kept, (192, 128)),
        scalars=2,
    )
    owners, sharers = ffd_groups()
    got = lax.all_to_all(windows, ALL, 0, 0, axis_index_groups=owners, tiled=True)
    chunks = call(place_kernel, shape(8, 72, 128), (got.reshape(WINDOWS * SLOT, 128),), scratch=((3, 256, 512),))
    got = lax.all_to_all(chunks, ALL, 0, 0, axis_index_groups=sharers, tiled=True)
    grad = call(sum_kernel, shape(3, 1, 3072), (got,), scratch=((72, 128),))
    return final, grad.reshape(1, 3, 3072)


def solution(mesh):
    placed = (
        P(None, "span", "chord", "normal"),
        P(None, None, None, "span", "chord", "normal"),
        P(),
        P("span", "chord"),
        P(),
        P(None, "span", "chord", "normal"),
        P("span", "chord", "normal"),
        P("span", "chord", "normal", None),
    )
    return jax.shard_map(
        local,
        mesh=mesh,
        in_specs=placed,
        out_specs=(P(None, "span", "chord", "normal"), P("span", None, ("chord", "normal"))),
        check_vma=False,
    )
```

```python
import math

import jax
import jax.numpy as jnp
import numpy as np
from jax import lax
from jax.experimental import pallas as pl
from jax.experimental.pallas import tpu as pltpu
from jax.sharding import PartitionSpec as P

F32 = jnp.float32
HIGHEST = lax.Precision.HIGHEST
ALL = ("span", "chord", "normal")
CX, CY, CZ = 8, 8, 128
LA = 96
ROWS = LA // 16
SLOT = 16
WINDOWS = 32


def bernstein(count, cells):
    degree = count - 1
    u = (np.arange(cells) + 0.5) / cells
    return np.stack([math.comb(degree, a) * u**a * (1 - u) ** (degree - a) for a in range(count)])


def tables():
    bx, by, bz = bernstein(8, CX), bernstein(8, CY), bernstein(8, CZ)
    along_z = np.zeros((CZ, 8, 2, 8))
    along_z[:] = bz.T[:, None, None, :]
    along_y = np.repeat(by.T, 16, axis=1)
    along_x = np.zeros((2, 4, 4, 3, CX, CY))
    for r in range(3):
        along_x[:, r, :, r] = 8.0 * bx.reshape(2, 4, CX)[..., None]
    return (
        along_z.reshape(CZ, 128).astype(np.float32),
        along_y.astype(np.float32),
        along_x.reshape(32, 192).astype(np.float32),
    )


def iotas():
    lane = lax.broadcasted_iota(jnp.int32, (8, 128), 1)
    row = lax.broadcasted_iota(jnp.int32, (8, 128), 0)
    return lane, row


def odd(axis):
    return lax.rem(lax.axis_index(axis), 2) == 1


def pick(flag, one, two):
    return jnp.where(jnp.full(one.shape, flag), one, two)


def pack(tile_of, fields, sends):
    lane, _ = iotas()
    xa, xb, ya, yb, za, zb = sends
    by_x, by_y, by_z = odd("span"), odd("chord"), odd("normal")
    low = jnp.zeros((8, 128), F32)
    high = jnp.zeros((8, 128), F32)
    for v in range(fields):
        first, last = tile_of(v, 0), tile_of(v, CX - 1)
        xa[v] = pick(by_x, first, last)
        xb[v] = pick(by_x, last, first)
        for x in range(CX):
            tile = tile_of(v, x)
            k = v * CX + x
            ya[k : k + 1, :] = pick(by_y, tile[0:1, :], tile[7:8, :])
            yb[k : k + 1, :] = pick(by_y, tile[7:8, :], tile[0:1, :])
            low = jnp.where(lane == k, pltpu.roll(tile, k, 1) if k else tile, low)
            high = jnp.where(lane == k, pltpu.roll(tile, k + 1, 1), high)
    za[...] = pick(by_z, low, high)
    zb[...] = pick(by_z, high, low)


def inner(axis, low, high):
    at = lax.axis_index(axis)
    last = lax.axis_size(axis) - 1
    zero = jnp.zeros(low.shape, F32)
    return pick(at > 0, low, zero), pick(at < last, high, zero)


def unpack(halo, planes_ref, rows_ref):
    xa, xb, ya, yb, za, zb = (one[...] for one in halo)
    by_x, by_y, by_z = odd("span"), odd("chord"), odd("normal")
    planes_ref[0], planes_ref[1] = inner("span", pick(by_x, xa, xb), pick(by_x, xb, xa))
    rows_ref[0], rows_ref[1] = inner("chord", pick(by_y, ya, yb), pick(by_y, yb, ya))
    return inner("normal", pick(by_z, za, zb), pick(by_z, zb, za))


def neighbour(e, tile_of, v, x, planes_ref, rows_ref, low, high):
    lane, row = iotas()
    k = v * CX + x
    if e == 1:
        return planes_ref[0, v] if x == 0 else tile_of(v, x - 1)
    if e == 2:
        return planes_ref[1, v] if x == CX - 1 else tile_of(v, x + 1)
    tile = tile_of(v, x)
    if e == 0:
        return tile
    if e == 3:
        return jnp.where(row == 0, rows_ref[0, k : k + 1, :], pltpu.roll(tile, 1, 0))
    if e == 4:
        return jnp.where(row == 7, rows_ref[1, k : k + 1, :], pltpu.roll(tile, 7, 0))
    if e == 5:
        return jnp.where(lane == 0, pltpu.roll(low, (128 - k) % 128, 1) if k else low, pltpu.roll(tile, 1, 1))
    return jnp.where(lane == 127, pltpu.roll(high, 127 - k, 1), pltpu.roll(tile, 127, 1))


def edges_kernel(adjoint_any, *refs):
    sends, (adjoint_ref, sem) = refs[:6], refs[6:]
    fetch = pltpu.make_async_copy(adjoint_any, adjoint_ref, sem)
    fetch.start()
    fetch.wait()
    pack(lambda v, x: adjoint_ref[v, x], 5, sends)


def flux_kernel(wall_any, map_any, adjoint_any, jacobian_any, face_any, stiff_any, *refs):
    halo, out_ref, sends = refs[:6], refs[6], refs[7:13]
    wall_ref, map_ref, adjoint_ref, jacobian_ref, face_ref, stiff_ref, total_ref, planes_ref, rows_ref, sems = refs[13:]
    copies = [
        pltpu.make_async_copy(wall_any, wall_ref, sems.at[0]),
        pltpu.make_async_copy(map_any, map_ref, sems.at[1]),
        pltpu.make_async_copy(adjoint_any, adjoint_ref, sems.at[2]),
        pltpu.make_async_copy(face_any, face_ref, sems.at[3]),
        pltpu.make_async_copy(stiff_any, stiff_ref, sems.at[4]),
    ]
    parts = [pltpu.make_async_copy(jacobian_any.at[e], jacobian_ref.at[e], sems.at[5 + e]) for e in range(7)]
    for copy in (copies[2], *parts, *copies[:2], copies[3], copies[4]):
        copy.start()
    lane, _ = iotas()
    on_wall = (lane == 0) & (lax.axis_index("normal") == 0)
    low, high = unpack(halo, planes_ref, rows_ref)
    tile_of = lambda v, x: adjoint_ref[v, x]
    copies[2].wait()
    for e in range(7):
        parts[e].wait()
        for x in range(CX):
            views = [neighbour(e, tile_of, p, x, planes_ref, rows_ref, low, high) for p in range(5)]
            total = [jnp.zeros((8, 128), F32) if e == 0 else total_ref[q, x] for q in range(5)]
            for p in range(5):
                for q in range(5):
                    total[q] = total[q] + jacobian_ref[e, p, q, x].astype(F32) * views[p]
            for q in range(5):
                total_ref[q, x] = total[q]
    for copy in (*copies[:2], *copies[3:]):
        copy.wait()
    square = lax.broadcasted_iota(jnp.int32, (8, 8), 0) == lax.broadcasted_iota(jnp.int32, (8, 8), 1)
    for x in range(CX):
        total = [total_ref[q, x] for q in range(5)]
        faces = jnp.broadcast_to(face_ref[x : x + 1, :], (8, 8)).astype(F32)
        face = jnp.sum(jnp.where(square, faces, 0.0), axis=1, keepdims=True)
        face = jnp.broadcast_to(face, (8, 128))
        for t in range(3):
            mask = on_wall & (face == float(t))
            for p in range(5):
                part = jnp.where(mask, adjoint_ref[p, x], 0.0)
                for q in range(5):
                    total[q] = total[q] + wall_ref[p, t, q] * part
        inverse = inverse_diagonal(stiff_ref, x)
        for r in range(3):
            sens = map_ref[r, 0] * total[0]
            for q in range(1, 5):
                sens = sens + map_ref[r, q] * total[q]
            out_ref[r, x] = sens * inverse
    pack(lambda v, x: out_ref[v, x], 3, sends)


def inverse_diagonal(stiff_ref, x):
    diagonal = stiff_ref[0, x]
    for e in range(1, 7):
        diagonal = diagonal + stiff_ref[e, x]
    return 1.0 / diagonal


def sweep(now_ref, start_ref, stiff_ref, halo, planes_ref, rows_ref, store):
    low, high = unpack(halo, planes_ref, rows_ref)
    tile_of = lambda v, x: now_ref[v, x]
    for x in range(CX):
        inverse = inverse_diagonal(stiff_ref, x)
        for v in range(3):
            total = stiff_ref[1, x] * neighbour(1, tile_of, v, x, planes_ref, rows_ref, low, high)
            for e in range(2, 7):
                total = total + stiff_ref[e, x] * neighbour(e, tile_of, v, x, planes_ref, rows_ref, low, high)
            store(v, x, start_ref[v, x] + total * inverse)


def middle_kernel(start_ref, stiff_ref, *refs):
    halo, out_ref, sends, planes_ref, rows_ref = refs[:6], refs[6], refs[7:13], *refs[13:]

    def store(v, x, tile):
        out_ref[v, x] = tile

    sweep(start_ref, start_ref, stiff_ref, halo, planes_ref, rows_ref, store)
    pack(lambda v, x: out_ref[v, x], 3, sends)


def window_kernel(box_ref, corner_ref, now_ref, start_ref, stiff_ref, bz_ref, by_ref, bx_ref, *refs):
    halo, out_ref, send_ref, planes_ref, rows_ref, flat_ref = refs[:6], *refs[6:]

    def store(v, x, tile):
        out_ref[v, x] = tile
        base = (v * CX + x) * CY
        flat_ref[base : base + CY, :] = tile

    sweep(now_ref, start_ref, stiff_ref, halo, planes_ref, rows_ref, store)
    inner = jnp.dot(flat_ref[...], bz_ref[...], precision=HIGHEST, preferred_element_type=F32)
    inner = inner * jnp.concatenate([by_ref[...]] * 24, axis=0)
    window = jnp.dot(bx_ref[...], inner, precision=HIGHEST, preferred_element_type=F32)
    lane = lax.broadcasted_iota(jnp.int32, (SLOT, 128), 1)
    row = lax.broadcasted_iota(jnp.int32, (SLOT, 128), 0)
    box = box_ref[0]
    oa, ob, oc = corner_ref[0], corner_ref[1], corner_ref[2]
    window = jnp.where(lax.rem(lane, 16) < 8, window[0:SLOT], window[SLOT : 2 * SLOT])
    shift = oc + 16 * lax.rem(ob, 8)
    window = pltpu.roll(window, shift, 1)
    inside = lax.rem(lane - shift + 128, 16) < 8
    block = jnp.where(inside, lax.div(ob, 8) + jnp.where(lane < shift, 1, 0), -1)
    for s in range(16):
        where = jnp.where(box == s, block, -1)
        there = jnp.where(row == 12, where, oa).astype(F32)
        there = jnp.where(row < 12, window, there)
        send_ref[2 * s] = there
        send_ref[2 * s + 1] = there


def place_kernel(got_ref, send_ref, wide_ref):
    half = lax.div(lax.axis_index("normal"), 2)
    where = got_ref[pl.ds(12, WINDOWS, stride=SLOT), :]
    start = got_ref[pl.ds(13, WINDOWS, stride=SLOT), :]
    lane = lax.broadcasted_iota(jnp.int32, (WINDOWS, 128), 1)
    row = lax.broadcasted_iota(jnp.int32, (WINDOWS, 128), 0)
    start = jnp.sum(jnp.where(lax.rem(lane, WINDOWS) == row, start, 0.0), axis=0, keepdims=True)
    step = lax.div(lax.broadcasted_iota(jnp.int32, (1, 128), 1), WINDOWS).astype(F32)
    first = start + step
    line = lax.broadcasted_iota(jnp.int32, (64, 128), 0)
    chunk = lax.div(line, 8)
    owner = lax.div(chunk, 2) * 4 + half * 2 + lax.rem(chunk, 2)
    point = jnp.where(lax.rem(line, 8) < ROWS, owner * ROWS + lax.rem(line, 8), -1).astype(F32)
    hits = jnp.concatenate(
        [jnp.where(point == jnp.broadcast_to(first + 4.0 * h, (64, 128)), 1.0, 0.0) for h in range(2)], axis=1
    )
    masks = [where == float(block) for block in range(4)]
    for r in range(3):
        for a in range(4):
            tile = got_ref[pl.ds(r * 4 + a, WINDOWS, stride=SLOT), :]
            for h in range(2):
                base = (h * 4 + a) * WINDOWS
                view = pltpu.roll(tile, 120, 1) if h else tile
                for block in range(4):
                    wide_ref[r, base : base + WINDOWS, block * 128 : block * 128 + 128] = jnp.where(
                        masks[block], view, 0.0
                    )
        placed = jnp.dot(hits, wide_ref[r], precision=HIGHEST, preferred_element_type=F32)
        for i in range(8):
            for block in range(4):
                base = (r * 4 + block) * ROWS
                send_ref[i, base : base + ROWS, :] = placed[
                    i * 8 : i * 8 + ROWS, block * 128 : block * 128 + 128
                ]


def sum_kernel(got_ref, out_ref, total_ref):
    total = got_ref[0]
    for j in range(1, 8):
        total = total + got_ref[j]
    total_ref[...] = total
    for r in range(3):
        for block in range(4):
            for a in range(ROWS):
                base = a * 512 + block * 128
                at = (r * 4 + block) * ROWS + a
                out_ref[r, 0:1, base : base + 128] = total_ref[at : at + 1, :]


VMEM = pl.BlockSpec(memory_space=pltpu.VMEM)
SMEM = pl.BlockSpec(memory_space=pltpu.SMEM)


def shape(*dims):
    return jax.ShapeDtypeStruct(dims, F32)


def call(body, outs, ins, scratch=(), scalars=0, limit=24 << 20, remote=()):
    specs = [SMEM] * scalars + [VMEM] * (len(ins) - scalars)
    for at in remote:
        specs[at] = HBM
    return pl.pallas_call(
        body,
        out_shape=outs,
        in_specs=specs,
        out_specs=jax.tree.map(lambda _: VMEM, outs),
        scratch_shapes=[pltpu.VMEM(a, F32) if isinstance(a, tuple) else a for a in scratch],
        compiler_params=pltpu.CompilerParams(vmem_limit_bytes=limit),
    )(*ins)


def in_hbm(one):
    return pltpu.with_memory_space_constraint(one, pltpu.HBM)


HBM = pl.BlockSpec(memory_space=pltpu.HBM)
DMA = pltpu.SemaphoreType.DMA


AXES = {"s": "span", "c": "chord", "n": "normal"}


def pairing(axis, start):
    count = lax.axis_size(axis)
    pairs = [(i, (i + 1) % count) for i in range(start, count, 2)]
    return pairs + [(j, i) for i, j in pairs]


def swap(*sends):
    got = []
    for at, one in enumerate(sends):
        name = "scn"[at // 2]
        got.append(lax.ppermute(one, AXES[name], pairing(AXES[name], at % 2)))
    return got


def ffd_groups():
    index = np.arange(256).reshape(16, 4, 2, 2)
    owners = index.transpose(1, 3, 0, 2).reshape(8, 32).tolist()
    sharers = index.transpose(0, 2, 1, 3).reshape(32, 8).tolist()
    return owners, sharers


def ends(v):
    return (shape(v, 8, 128),) * 2 + (shape(v * 8, 128),) * 2 + (shape(8, 128),) * 2


def local(adjoint, jacobian, wall_table, face_type, mesh_map, stiffness, box_map, offsets):
    block = shape(3, CX, CY, CZ)
    out = call(edges_kernel, ends(5), (in_hbm(adjoint),), scratch=((5, CX, CY, CZ), DMA), remote=(0,))
    halo = swap(*out)
    fixed = (wall_table.transpose(1, 0, 2), mesh_map, adjoint, jacobian, face_type, stiffness)
    spaces = (pltpu.SMEM, pltpu.SMEM) + (pltpu.VMEM,) * 4
    start, *out = call(
        flux_kernel,
        (block, *ends(3)),
        (*map(in_hbm, fixed), *halo),
        scratch=(
            *(space(one.shape, one.dtype) for space, one in zip(spaces, fixed)),
            (5, CX, CY, CZ),
            (2, 5, 8, 128),
            (2, 40, 128),
            DMA((12,)),
        ),
        remote=range(6),
    )
    halo = swap(*out)
    kept = ((2, 3, 8, 128), (2, 24, 128))
    middle, *out = call(middle_kernel, (block, *ends(3)), (start, stiffness, *halo), scratch=kept)
    halo = swap(*out)
    bz, by, bx = tables()
    final, windows = call(
        window_kernel,
        (block, shape(WINDOWS, SLOT, 128)),
        (box_map.reshape(1), offsets.reshape(3), middle, start, stiffness, bz, by, bx, *halo),
        scratch=(*kept, (192, 128)),
        scalars=2,
    )
    owners, sharers = ffd_groups()
    got = lax.all_to_all(windows, ALL, 0, 0, axis_index_groups=owners, tiled=True)
    chunks = call(place_kernel, shape(8, 72, 128), (got.reshape(WINDOWS * SLOT, 128),), scratch=((3, 256, 512),))
    got = lax.all_to_all(chunks, ALL, 0, 0, axis_index_groups=sharers, tiled=True)
    grad = call(sum_kernel, shape(3, 1, 3072), (got,), scratch=((72, 128),))
    return final, grad.reshape(1, 3, 3072)


def solution(mesh):
    placed = (
        P(None, "span", "chord", "normal"),
        P(None, None, None, "span", "chord", "normal"),
        P(),
        P("span", "chord"),
        P(),
        P(None, "span", "chord", "normal"),
        P("span", "chord", "normal"),
        P("span", "chord", "normal", None),
    )
    return jax.shard_map(
        local,
        mesh=mesh,
        in_specs=placed,
        out_specs=(P(None, "span", "chord", "normal"), P("span", None, ("chord", "normal"))),
        check_vma=False,
    )
```

```python
import math

import jax
import jax.numpy as jnp
import numpy as np
from jax import lax
from jax.experimental import pallas as pl
from jax.experimental.pallas import tpu as pltpu
from jax.sharding import PartitionSpec as P

F32 = jnp.float32
HIGHEST = lax.Precision.HIGHEST
ALL = ("span", "chord", "normal")
CX, CY, CZ = 8, 8, 128
LA = 96
ROWS = LA // 16
SLOT = 16
WINDOWS = 32


def bernstein(count, cells):
    degree = count - 1
    u = (np.arange(cells) + 0.5) / cells
    return np.stack([math.comb(degree, a) * u**a * (1 - u) ** (degree - a) for a in range(count)])


def tables():
    bx, by, bz = bernstein(8, CX), bernstein(8, CY), bernstein(8, CZ)
    along_z = np.zeros((CZ, 8, 2, 8))
    along_z[:] = bz.T[:, None, None, :]
    along_y = np.repeat(by.T, 16, axis=1)
    along_x = np.zeros((2, 4, 4, 3, CX, CY))
    for r in range(3):
        along_x[:, r, :, r] = 8.0 * bx.reshape(2, 4, CX)[..., None]
    return (
        along_z.reshape(CZ, 128).astype(np.float32),
        along_y.astype(np.float32),
        along_x.reshape(32, 192).astype(np.float32),
    )


def iotas():
    lane = lax.broadcasted_iota(jnp.int32, (8, 128), 1)
    row = lax.broadcasted_iota(jnp.int32, (8, 128), 0)
    return lane, row


def odd(axis):
    return lax.rem(lax.axis_index(axis), 2) == 1


def pick(flag, one, two):
    return jnp.where(jnp.full(one.shape, flag), one, two)


def pack(tile_of, fields, sends):
    lane, _ = iotas()
    xa, xb, ya, yb, za, zb = sends
    by_x, by_y, by_z = odd("span"), odd("chord"), odd("normal")
    low = jnp.zeros((8, 128), F32)
    high = jnp.zeros((8, 128), F32)
    for v in range(fields):
        first, last = tile_of(v, 0), tile_of(v, CX - 1)
        xa[v] = pick(by_x, first, last)
        xb[v] = pick(by_x, last, first)
        for x in range(CX):
            tile = tile_of(v, x)
            k = v * CX + x
            ya[k : k + 1, :] = pick(by_y, tile[0:1, :], tile[7:8, :])
            yb[k : k + 1, :] = pick(by_y, tile[7:8, :], tile[0:1, :])
            low = jnp.where(lane == k, pltpu.roll(tile, k, 1) if k else tile, low)
            high = jnp.where(lane == k, pltpu.roll(tile, k + 1, 1), high)
    za[...] = pick(by_z, low, high)
    zb[...] = pick(by_z, high, low)


def inner(axis, low, high):
    at = lax.axis_index(axis)
    last = lax.axis_size(axis) - 1
    zero = jnp.zeros(low.shape, F32)
    return pick(at > 0, low, zero), pick(at < last, high, zero)


def unpack(halo, planes_ref, rows_ref):
    xa, xb, ya, yb, za, zb = (one[...] for one in halo)
    by_x, by_y, by_z = odd("span"), odd("chord"), odd("normal")
    planes_ref[0], planes_ref[1] = inner("span", pick(by_x, xa, xb), pick(by_x, xb, xa))
    rows_ref[0], rows_ref[1] = inner("chord", pick(by_y, ya, yb), pick(by_y, yb, ya))
    return inner("normal", pick(by_z, za, zb), pick(by_z, zb, za))


def neighbour(e, tile_of, v, x, planes_ref, rows_ref, low, high):
    lane, row = iotas()
    k = v * CX + x
    if e == 1:
        return planes_ref[0, v] if x == 0 else tile_of(v, x - 1)
    if e == 2:
        return planes_ref[1, v] if x == CX - 1 else tile_of(v, x + 1)
    tile = tile_of(v, x)
    if e == 0:
        return tile
    if e == 3:
        return jnp.where(row == 0, rows_ref[0, k : k + 1, :], pltpu.roll(tile, 1, 0))
    if e == 4:
        return jnp.where(row == 7, rows_ref[1, k : k + 1, :], pltpu.roll(tile, 7, 0))
    if e == 5:
        return jnp.where(lane == 0, pltpu.roll(low, (128 - k) % 128, 1) if k else low, pltpu.roll(tile, 1, 1))
    return jnp.where(lane == 127, pltpu.roll(high, 127 - k, 1), pltpu.roll(tile, 127, 1))


def edges_kernel(adjoint_any, *refs):
    sends, (adjoint_ref, sem) = refs[:6], refs[6:]
    fetch = pltpu.make_async_copy(adjoint_any, adjoint_ref, sem)
    fetch.start()
    fetch.wait()
    pack(lambda v, x: adjoint_ref[v, x], 5, sends)


def flux_kernel(wall_any, map_any, adjoint_any, jacobian_any, face_any, stiff_any, *refs):
    halo, out_ref, sends = refs[:6], refs[6], refs[7:13]
    wall_ref, map_ref, adjoint_ref, jacobian_ref, face_ref, stiff_ref, total_ref, planes_ref, rows_ref, sems = refs[13:]
    copies = [
        pltpu.make_async_copy(wall_any, wall_ref, sems.at[0]),
        pltpu.make_async_copy(map_any, map_ref, sems.at[1]),
        pltpu.make_async_copy(adjoint_any, adjoint_ref, sems.at[2]),
        pltpu.make_async_copy(face_any, face_ref, sems.at[3]),
        pltpu.make_async_copy(stiff_any, stiff_ref, sems.at[4]),
    ]
    parts = [pltpu.make_async_copy(jacobian_any.at[e], jacobian_ref.at[e], sems.at[5 + e]) for e in range(7)]
    for copy in (copies[2], *parts, *copies[:2], copies[3], copies[4]):
        copy.start()
    lane, _ = iotas()
    on_wall = (lane == 0) & (lax.axis_index("normal") == 0)
    low, high = unpack(halo, planes_ref, rows_ref)
    tile_of = lambda v, x: adjoint_ref[v, x]
    copies[2].wait()
    for e in range(7):
        parts[e].wait()
        for x in range(CX):
            views = [neighbour(e, tile_of, p, x, planes_ref, rows_ref, low, high) for p in range(5)]
            total = [jnp.zeros((8, 128), F32) if e == 0 else total_ref[q, x] for q in range(5)]
            for p in range(5):
                for q in range(5):
                    total[q] = total[q] + jacobian_ref[e, p, q, x].astype(F32) * views[p]
            for q in range(5):
                total_ref[q, x] = total[q]
    for copy in (*copies[:2], *copies[3:]):
        copy.wait()
    square = lax.broadcasted_iota(jnp.int32, (8, 8), 0) == lax.broadcasted_iota(jnp.int32, (8, 8), 1)
    for x in range(CX):
        total = [total_ref[q, x] for q in range(5)]
        faces = jnp.broadcast_to(face_ref[x : x + 1, :], (8, 8)).astype(F32)
        face = jnp.sum(jnp.where(square, faces, 0.0), axis=1, keepdims=True)
        face = jnp.broadcast_to(face, (8, 128))
        for t in range(3):
            mask = on_wall & (face == float(t))
            for p in range(5):
                part = jnp.where(mask, adjoint_ref[p, x], 0.0)
                for q in range(5):
                    total[q] = total[q] + wall_ref[p, t, q] * part
        inverse = inverse_diagonal(stiff_ref, x)
        for r in range(3):
            sens = map_ref[r, 0] * total[0]
            for q in range(1, 5):
                sens = sens + map_ref[r, q] * total[q]
            out_ref[r, x] = sens * inverse
    pack(lambda v, x: out_ref[v, x], 3, sends)


def inverse_diagonal(stiff_ref, x):
    diagonal = stiff_ref[0, x]
    for e in range(1, 7):
        diagonal = diagonal + stiff_ref[e, x]
    return 1.0 / diagonal


def sweep(now_ref, start_ref, stiff_ref, halo, planes_ref, rows_ref, store):
    low, high = unpack(halo, planes_ref, rows_ref)
    tile_of = lambda v, x: now_ref[v, x]
    for x in range(CX):
        inverse = inverse_diagonal(stiff_ref, x)
        for v in range(3):
            total = stiff_ref[1, x] * neighbour(1, tile_of, v, x, planes_ref, rows_ref, low, high)
            for e in range(2, 7):
                total = total + stiff_ref[e, x] * neighbour(e, tile_of, v, x, planes_ref, rows_ref, low, high)
            store(v, x, start_ref[v, x] + total * inverse)


def middle_kernel(start_ref, stiff_ref, *refs):
    halo, out_ref, sends, planes_ref, rows_ref = refs[:6], refs[6], refs[7:13], *refs[13:]

    def store(v, x, tile):
        out_ref[v, x] = tile

    sweep(start_ref, start_ref, stiff_ref, halo, planes_ref, rows_ref, store)
    pack(lambda v, x: out_ref[v, x], 3, sends)


def window_kernel(box_ref, corner_ref, now_ref, start_ref, stiff_ref, bz_ref, by_ref, bx_ref, *refs):
    halo, out_ref, send_ref, planes_ref, rows_ref, flat_ref = refs[:6], *refs[6:]

    def store(v, x, tile):
        out_ref[v, x] = tile
        base = (v * CX + x) * CY
        flat_ref[base : base + CY, :] = tile

    sweep(now_ref, start_ref, stiff_ref, halo, planes_ref, rows_ref, store)
    inner = jnp.dot(flat_ref[...], bz_ref[...], precision=HIGHEST, preferred_element_type=F32)
    inner = inner * jnp.concatenate([by_ref[...]] * 24, axis=0)
    window = jnp.dot(bx_ref[...], inner, precision=HIGHEST, preferred_element_type=F32)
    lane = lax.broadcasted_iota(jnp.int32, (SLOT, 128), 1)
    row = lax.broadcasted_iota(jnp.int32, (SLOT, 128), 0)
    box = box_ref[0]
    oa, ob, oc = corner_ref[0], corner_ref[1], corner_ref[2]
    window = jnp.where(lax.rem(lane, 16) < 8, window[0:SLOT], window[SLOT : 2 * SLOT])
    shift = oc + 16 * lax.rem(ob, 8)
    window = pltpu.roll(window, shift, 1)
    inside = lax.rem(lane - shift + 128, 16) < 8
    block = jnp.where(inside, lax.div(ob, 8) + jnp.where(lane < shift, 1, 0), -1)
    for s in range(16):
        where = jnp.where(box == s, block, -1)
        there = jnp.where(row == 12, where, oa).astype(F32)
        there = jnp.where(row < 12, window, there)
        send_ref[2 * s] = there
        send_ref[2 * s + 1] = there


def place_kernel(got_ref, *refs):
    keep_ref, give_ref, wide_ref, chunk_ref = refs
    half = lax.div(lax.axis_index("normal"), 2)
    where = got_ref[pl.ds(12, WINDOWS, stride=SLOT), :]
    start = got_ref[pl.ds(13, WINDOWS, stride=SLOT), :]
    lane = lax.broadcasted_iota(jnp.int32, (WINDOWS, 128), 1)
    row = lax.broadcasted_iota(jnp.int32, (WINDOWS, 128), 0)
    start = jnp.sum(jnp.where(lax.rem(lane, WINDOWS) == row, start, 0.0), axis=0, keepdims=True)
    step = lax.div(lax.broadcasted_iota(jnp.int32, (1, 128), 1), WINDOWS).astype(F32)
    first = start + step
    line = lax.broadcasted_iota(jnp.int32, (64, 128), 0)
    chunk = lax.div(line, 8)
    owner = lax.div(chunk, 2) * 4 + half * 2 + lax.rem(chunk, 2)
    point = jnp.where(lax.rem(line, 8) < ROWS, owner * ROWS + lax.rem(line, 8), -1).astype(F32)
    hits = jnp.concatenate(
        [jnp.where(point == jnp.broadcast_to(first + 4.0 * h, (64, 128)), 1.0, 0.0) for h in range(2)], axis=1
    )
    masks = [where == float(block) for block in range(4)]
    for r in range(3):
        for a in range(4):
            tile = got_ref[pl.ds(r * 4 + a, WINDOWS, stride=SLOT), :]
            for h in range(2):
                base = (h * 4 + a) * WINDOWS
                view = pltpu.roll(tile, 120, 1) if h else tile
                for block in range(4):
                    wide_ref[r, base : base + WINDOWS, block * 128 : block * 128 + 128] = jnp.where(
                        masks[block], view, 0.0
                    )
        placed = jnp.dot(hits, wide_ref[r], precision=HIGHEST, preferred_element_type=F32)
        for i in range(8):
            for block in range(4):
                base = (r * 4 + block) * ROWS
                chunk_ref[i, base : base + ROWS, :] = placed[
                    i * 8 : i * 8 + ROWS, block * 128 : block * 128 + 128
                ]
    near = lax.rem(lax.axis_index("normal"), 2)
    for c in range(4):
        keep_ref[c] = chunk_ref[c * 2 + near]
        give_ref[c] = chunk_ref[c * 2 + 1 - near]


def join_kernel(keep_ref, got_ref, *sends):
    mine = lax.axis_index("chord")
    for d in range(4):
        at = lax.bitwise_xor(mine, d)
        sends[d][...] = keep_ref[at] + got_ref[at]


def sum_kernel(*refs):
    got, (out_ref, total_ref) = refs[:4], refs[4:]
    total = got[0][...]
    for one in got[1:]:
        total = total + one[...]
    total_ref[...] = total
    for r in range(3):
        for block in range(4):
            for a in range(ROWS):
                base = a * 512 + block * 128
                at = (r * 4 + block) * ROWS + a
                out_ref[r, 0:1, base : base + 128] = total_ref[at : at + 1, :]


VMEM = pl.BlockSpec(memory_space=pltpu.VMEM)
SMEM = pl.BlockSpec(memory_space=pltpu.SMEM)


def shape(*dims):
    return jax.ShapeDtypeStruct(dims, F32)


def call(body, outs, ins, scratch=(), scalars=0, limit=24 << 20, remote=()):
    specs = [SMEM] * scalars + [VMEM] * (len(ins) - scalars)
    for at in remote:
        specs[at] = HBM
    return pl.pallas_call(
        body,
        out_shape=outs,
        in_specs=specs,
        out_specs=jax.tree.map(lambda _: VMEM, outs),
        scratch_shapes=[pltpu.VMEM(a, F32) if isinstance(a, tuple) else a for a in scratch],
        compiler_params=pltpu.CompilerParams(vmem_limit_bytes=limit),
    )(*ins)


def in_hbm(one):
    return pltpu.with_memory_space_constraint(one, pltpu.HBM)


HBM = pl.BlockSpec(memory_space=pltpu.HBM)
DMA = pltpu.SemaphoreType.DMA


AXES = {"s": "span", "c": "chord", "n": "normal"}


def pairing(axis, start):
    count = lax.axis_size(axis)
    pairs = [(i, (i + 1) % count) for i in range(start, count, 2)]
    return pairs + [(j, i) for i, j in pairs]


def swap(*sends):
    got = []
    for at, one in enumerate(sends):
        name = "scn"[at // 2]
        got.append(lax.ppermute(one, AXES[name], pairing(AXES[name], at % 2)))
    return got


def owners():
    index = np.arange(256).reshape(16, 4, 2, 2)
    return index.transpose(1, 3, 0, 2).reshape(8, 32).tolist()


def ends(v):
    return (shape(v, 8, 128),) * 2 + (shape(v * 8, 128),) * 2 + (shape(8, 128),) * 2


def local(adjoint, jacobian, wall_table, face_type, mesh_map, stiffness, box_map, offsets):
    block = shape(3, CX, CY, CZ)
    out = call(edges_kernel, ends(5), (in_hbm(adjoint),), scratch=((5, CX, CY, CZ), DMA), remote=(0,))
    halo = swap(*out)
    fixed = (wall_table.transpose(1, 0, 2), mesh_map, adjoint, jacobian, face_type, stiffness)
    spaces = (pltpu.SMEM, pltpu.SMEM) + (pltpu.VMEM,) * 4
    start, *out = call(
        flux_kernel,
        (block, *ends(3)),
        (*map(in_hbm, fixed), *halo),
        scratch=(
            *(space(one.shape, one.dtype) for space, one in zip(spaces, fixed)),
            (5, CX, CY, CZ),
            (2, 5, 8, 128),
            (2, 40, 128),
            DMA((12,)),
        ),
        remote=range(6),
    )
    halo = swap(*out)
    kept = ((2, 3, 8, 128), (2, 24, 128))
    middle, *out = call(middle_kernel, (block, *ends(3)), (start, stiffness, *halo), scratch=kept)
    halo = swap(*out)
    bz, by, bx = tables()
    final, windows = call(
        window_kernel,
        (block, shape(WINDOWS, SLOT, 128)),
        (box_map.reshape(1), offsets.reshape(3), middle, start, stiffness, bz, by, bx, *halo),
        scratch=(*kept, (192, 128)),
        scalars=2,
    )
    got = lax.all_to_all(windows, ALL, 0, 0, axis_index_groups=owners(), tiled=True)
    keep, give = call(
        place_kernel,
        (shape(4, 72, 128),) * 2,
        (got.reshape(WINDOWS * SLOT, 128),),
        scratch=((3, 256, 512), (8, 72, 128)),
    )
    got = lax.ppermute(give, "normal", pairing("normal", 0))
    mine, *chunks = call(join_kernel, (shape(72, 128),) * 4, (keep, got))
    got = [lax.ppermute(one, "chord", [(i, i ^ d) for i in range(4)]) for d, one in enumerate(chunks, 1)]
    grad = call(sum_kernel, shape(3, 1, 3072), (mine, *got), scratch=((72, 128),))
    return final, grad.reshape(1, 3, 3072)


def solution(mesh):
    placed = (
        P(None, "span", "chord", "normal"),
        P(None, None, None, "span", "chord", "normal"),
        P(),
        P("span", "chord"),
        P(),
        P(None, "span", "chord", "normal"),
        P("span", "chord", "normal"),
        P("span", "chord", "normal", None),
    )
    return jax.shard_map(
        local,
        mesh=mesh,
        in_specs=placed,
        out_specs=(P(None, "span", "chord", "normal"), P("span", None, ("chord", "normal"))),
        check_vma=False,
    )
```

```python
import math

import jax
import jax.numpy as jnp
import numpy as np
from jax import lax
from jax.experimental import pallas as pl
from jax.experimental.pallas import tpu as pltpu
from jax.sharding import PartitionSpec as P

F32 = jnp.float32
HIGHEST = lax.Precision.HIGHEST
ALL = ("span", "chord", "normal")
CX, CY, CZ = 8, 8, 128
LA = 96
ROWS = LA // 16
SLOT = 16
WINDOWS = 32


def bernstein(count, cells):
    degree = count - 1
    u = (np.arange(cells) + 0.5) / cells
    return np.stack([math.comb(degree, a) * u**a * (1 - u) ** (degree - a) for a in range(count)])


def tables():
    bx, by, bz = bernstein(8, CX), bernstein(8, CY), bernstein(8, CZ)
    along_z = np.zeros((CZ, 8, 2, 8))
    along_z[:] = bz.T[:, None, None, :]
    along_y = np.repeat(by.T, 16, axis=1)
    along_x = np.zeros((2, 4, 4, 3, CX, CY))
    for r in range(3):
        along_x[:, r, :, r] = 8.0 * bx.reshape(2, 4, CX)[..., None]
    return (
        along_z.reshape(CZ, 128).astype(np.float32),
        along_y.astype(np.float32),
        along_x.reshape(32, 192).astype(np.float32),
    )


def iotas():
    lane = lax.broadcasted_iota(jnp.int32, (8, 128), 1)
    row = lax.broadcasted_iota(jnp.int32, (8, 128), 0)
    return lane, row


def odd(axis):
    return lax.rem(lax.axis_index(axis), 2) == 1


def pick(flag, one, two):
    return jnp.where(jnp.full(one.shape, flag), one, two)


def pack(tile_of, fields, sends):
    lane, _ = iotas()
    xa, xb, ya, yb, za, zb = sends
    by_x, by_y, by_z = odd("span"), odd("chord"), odd("normal")
    low = jnp.zeros((8, 128), F32)
    high = jnp.zeros((8, 128), F32)
    for v in range(fields):
        first, last = tile_of(v, 0), tile_of(v, CX - 1)
        xa[v] = pick(by_x, first, last)
        xb[v] = pick(by_x, last, first)
        for x in range(CX):
            tile = tile_of(v, x)
            k = v * CX + x
            ya[k : k + 1, :] = pick(by_y, tile[0:1, :], tile[7:8, :])
            yb[k : k + 1, :] = pick(by_y, tile[7:8, :], tile[0:1, :])
            low = jnp.where(lane == k, pltpu.roll(tile, k, 1) if k else tile, low)
            high = jnp.where(lane == k, pltpu.roll(tile, k + 1, 1), high)
    za[...] = pick(by_z, low, high)
    zb[...] = pick(by_z, high, low)


def inner(axis, low, high):
    at = lax.axis_index(axis)
    last = lax.axis_size(axis) - 1
    zero = jnp.zeros(low.shape, F32)
    return pick(at > 0, low, zero), pick(at < last, high, zero)


def unpack(halo, planes_ref, rows_ref):
    xa, xb, ya, yb, za, zb = (one[...] for one in halo)
    by_x, by_y, by_z = odd("span"), odd("chord"), odd("normal")
    planes_ref[0], planes_ref[1] = inner("span", pick(by_x, xa, xb), pick(by_x, xb, xa))
    rows_ref[0], rows_ref[1] = inner("chord", pick(by_y, ya, yb), pick(by_y, yb, ya))
    return inner("normal", pick(by_z, za, zb), pick(by_z, zb, za))


def neighbour(e, tile_of, v, x, planes_ref, rows_ref, low, high):
    lane, row = iotas()
    k = v * CX + x
    if e == 1:
        return planes_ref[0, v] if x == 0 else tile_of(v, x - 1)
    if e == 2:
        return planes_ref[1, v] if x == CX - 1 else tile_of(v, x + 1)
    tile = tile_of(v, x)
    if e == 0:
        return tile
    if e == 3:
        return jnp.where(row == 0, rows_ref[0, k : k + 1, :], pltpu.roll(tile, 1, 0))
    if e == 4:
        return jnp.where(row == 7, rows_ref[1, k : k + 1, :], pltpu.roll(tile, 7, 0))
    if e == 5:
        return jnp.where(lane == 0, pltpu.roll(low, (128 - k) % 128, 1) if k else low, pltpu.roll(tile, 1, 1))
    return jnp.where(lane == 127, pltpu.roll(high, 127 - k, 1), pltpu.roll(tile, 127, 1))


def edges_kernel(adjoint_any, *refs):
    sends, (adjoint_ref, sem) = refs[:6], refs[6:]
    fetch = pltpu.make_async_copy(adjoint_any, adjoint_ref, sem)
    fetch.start()
    fetch.wait()
    pack(lambda v, x: adjoint_ref[v, x], 5, sends)


def flux_kernel(wall_any, map_any, adjoint_any, jacobian_any, face_any, stiff_any, *refs):
    halo, out_ref, sends = refs[:6], refs[6], refs[7:13]
    wall_ref, map_ref, adjoint_ref, jacobian_ref, face_ref, stiff_ref, total_ref, planes_ref, rows_ref, sems = refs[13:]
    copies = [
        pltpu.make_async_copy(wall_any, wall_ref, sems.at[0]),
        pltpu.make_async_copy(map_any, map_ref, sems.at[1]),
        pltpu.make_async_copy(adjoint_any, adjoint_ref, sems.at[2]),
        pltpu.make_async_copy(face_any, face_ref, sems.at[3]),
        pltpu.make_async_copy(stiff_any, stiff_ref, sems.at[4]),
    ]
    parts = [pltpu.make_async_copy(jacobian_any.at[e], jacobian_ref.at[e], sems.at[5 + e]) for e in range(7)]
    for copy in (copies[2], *parts, *copies[:2], copies[3], copies[4]):
        copy.start()
    lane, _ = iotas()
    on_wall = (lane == 0) & (lax.axis_index("normal") == 0)
    low, high = unpack(halo, planes_ref, rows_ref)
    tile_of = lambda v, x: adjoint_ref[v, x]
    copies[2].wait()
    for e in range(7):
        parts[e].wait()
        for x in range(CX):
            views = [neighbour(e, tile_of, p, x, planes_ref, rows_ref, low, high) for p in range(5)]
            total = [jnp.zeros((8, 128), F32) if e == 0 else total_ref[q, x] for q in range(5)]
            for p in range(5):
                for q in range(5):
                    total[q] = total[q] + jacobian_ref[e, p, q, x].astype(F32) * views[p]
            for q in range(5):
                total_ref[q, x] = total[q]
    for copy in (*copies[:2], *copies[3:]):
        copy.wait()
    square = lax.broadcasted_iota(jnp.int32, (8, 8), 0) == lax.broadcasted_iota(jnp.int32, (8, 8), 1)
    for x in range(CX):
        total = [total_ref[q, x] for q in range(5)]
        faces = jnp.broadcast_to(face_ref[x : x + 1, :], (8, 8)).astype(F32)
        face = jnp.sum(jnp.where(square, faces, 0.0), axis=1, keepdims=True)
        face = jnp.broadcast_to(face, (8, 128))
        for t in range(3):
            mask = on_wall & (face == float(t))
            for p in range(5):
                part = jnp.where(mask, adjoint_ref[p, x], 0.0)
                for q in range(5):
                    total[q] = total[q] + wall_ref[p, t, q] * part
        inverse = inverse_diagonal(stiff_ref, x)
        for r in range(3):
            sens = map_ref[r, 0] * total[0]
            for q in range(1, 5):
                sens = sens + map_ref[r, q] * total[q]
            out_ref[r, x] = sens * inverse
    pack(lambda v, x: out_ref[v, x], 3, sends)


def inverse_diagonal(stiff_ref, x):
    diagonal = stiff_ref[0, x]
    for e in range(1, 7):
        diagonal = diagonal + stiff_ref[e, x]
    return 1.0 / diagonal


def sweep(now_ref, start_ref, stiff_ref, halo, planes_ref, rows_ref, store):
    low, high = unpack(halo, planes_ref, rows_ref)
    tile_of = lambda v, x: now_ref[v, x]
    for x in range(CX):
        inverse = inverse_diagonal(stiff_ref, x)
        for v in range(3):
            total = stiff_ref[1, x] * neighbour(1, tile_of, v, x, planes_ref, rows_ref, low, high)
            for e in range(2, 7):
                total = total + stiff_ref[e, x] * neighbour(e, tile_of, v, x, planes_ref, rows_ref, low, high)
            store(v, x, start_ref[v, x] + total * inverse)


def middle_kernel(start_ref, stiff_ref, *refs):
    halo, out_ref, sends, planes_ref, rows_ref = refs[:6], refs[6], refs[7:13], *refs[13:]

    def store(v, x, tile):
        out_ref[v, x] = tile

    sweep(start_ref, start_ref, stiff_ref, halo, planes_ref, rows_ref, store)
    pack(lambda v, x: out_ref[v, x], 3, sends)


def window_kernel(box_ref, corner_ref, now_ref, start_ref, stiff_ref, bz_ref, by_ref, bx_ref, *refs):
    halo, out_ref, send_ref, planes_ref, rows_ref, flat_ref = refs[:6], *refs[6:]

    def store(v, x, tile):
        out_ref[v, x] = tile
        base = (v * CX + x) * CY
        flat_ref[base : base + CY, :] = tile

    sweep(now_ref, start_ref, stiff_ref, halo, planes_ref, rows_ref, store)
    inner = jnp.dot(flat_ref[...], bz_ref[...], precision=HIGHEST, preferred_element_type=F32)
    inner = inner * jnp.concatenate([by_ref[...]] * 24, axis=0)
    window = jnp.dot(bx_ref[...], inner, precision=HIGHEST, preferred_element_type=F32)
    lane = lax.broadcasted_iota(jnp.int32, (SLOT, 128), 1)
    row = lax.broadcasted_iota(jnp.int32, (SLOT, 128), 0)
    box = box_ref[0]
    oa, ob, oc = corner_ref[0], corner_ref[1], corner_ref[2]
    window = jnp.where(lax.rem(lane, 16) < 8, window[0:SLOT], window[SLOT : 2 * SLOT])
    shift = oc + 16 * lax.rem(ob, 8)
    window = pltpu.roll(window, shift, 1)
    inside = lax.rem(lane - shift + 128, 16) < 8
    block = jnp.where(inside, lax.div(ob, 8) + jnp.where(lane < shift, 1, 0), -1)
    for s in range(16):
        where = jnp.where(box == s, block, -1)
        there = jnp.where(row == 12, where, oa).astype(F32)
        there = jnp.where(row < 12, window, there)
        send_ref[2 * s] = there
        send_ref[2 * s + 1] = there


def split(one, count):
    parts = []
    for _ in range(count):
        part = one.astype(jnp.bfloat16)
        parts.append(part)
        one = one - part.astype(F32)
    return parts


def place_kernel(got_ref, *refs):
    keep_ref, give_ref, wide_ref, chunk_ref = refs
    half = lax.div(lax.axis_index("normal"), 2)
    where = got_ref[pl.ds(12, WINDOWS, stride=SLOT), :]
    start = got_ref[pl.ds(13, WINDOWS, stride=SLOT), :]
    lane = lax.broadcasted_iota(jnp.int32, (WINDOWS, 128), 1)
    row = lax.broadcasted_iota(jnp.int32, (WINDOWS, 128), 0)
    start = jnp.sum(jnp.where(lax.rem(lane, WINDOWS) == row, start, 0.0), axis=0, keepdims=True)
    step = lax.div(lax.broadcasted_iota(jnp.int32, (1, 128), 1), WINDOWS).astype(F32)
    first = start + step
    line = lax.broadcasted_iota(jnp.int32, (64, 128), 0)
    chunk = lax.div(line, 8)
    owner = lax.div(chunk, 2) * 4 + half * 2 + lax.rem(chunk, 2)
    point = jnp.where(lax.rem(line, 8) < ROWS, owner * ROWS + lax.rem(line, 8), -1).astype(F32)
    hits = jnp.concatenate(
        [jnp.where(point == jnp.broadcast_to(first + 4.0 * h, (64, 128)), 1.0, 0.0) for h in range(2)], axis=1
    )
    hits = hits.astype(jnp.bfloat16)
    masks = [where == float(block) for block in range(4)]
    for r in range(3):
        for a in range(4):
            tile = got_ref[pl.ds(r * 4 + a, WINDOWS, stride=SLOT), :]
            for h in range(2):
                base = (h * 4 + a) * WINDOWS
                view = pltpu.roll(tile, 120, 1) if h else tile
                for block in range(4):
                    wide_ref[r, base : base + WINDOWS, block * 128 : block * 128 + 128] = jnp.where(
                        masks[block], view, 0.0
                    )
        placed = sum(jnp.dot(hits, part, preferred_element_type=F32) for part in split(wide_ref[r], 3))
        for i in range(8):
            for block in range(4):
                base = (r * 4 + block) * ROWS
                chunk_ref[i, base : base + ROWS, :] = placed[
                    i * 8 : i * 8 + ROWS, block * 128 : block * 128 + 128
                ]
    near = lax.rem(lax.axis_index("normal"), 2)
    for c in range(4):
        keep_ref[c] = chunk_ref[c * 2 + near]
        give_ref[c] = chunk_ref[c * 2 + 1 - near]


def join_kernel(keep_ref, got_ref, *sends):
    mine = lax.axis_index("chord")
    for d in range(4):
        at = lax.bitwise_xor(mine, d)
        sends[d][...] = keep_ref[at] + got_ref[at]


def sum_kernel(*refs):
    got, (out_ref, total_ref) = refs[:4], refs[4:]
    total = got[0][...]
    for one in got[1:]:
        total = total + one[...]
    total_ref[...] = total
    for r in range(3):
        for block in range(4):
            for a in range(ROWS):
                base = a * 512 + block * 128
                at = (r * 4 + block) * ROWS + a
                out_ref[r, 0:1, base : base + 128] = total_ref[at : at + 1, :]


VMEM = pl.BlockSpec(memory_space=pltpu.VMEM)
SMEM = pl.BlockSpec(memory_space=pltpu.SMEM)


def shape(*dims):
    return jax.ShapeDtypeStruct(dims, F32)


def call(body, outs, ins, scratch=(), scalars=0, limit=24 << 20, remote=()):
    specs = [SMEM] * scalars + [VMEM] * (len(ins) - scalars)
    for at in remote:
        specs[at] = HBM
    return pl.pallas_call(
        body,
        out_shape=outs,
        in_specs=specs,
        out_specs=jax.tree.map(lambda _: VMEM, outs),
        scratch_shapes=[pltpu.VMEM(a, F32) if isinstance(a, tuple) else a for a in scratch],
        compiler_params=pltpu.CompilerParams(vmem_limit_bytes=limit),
    )(*ins)


def in_hbm(one):
    return pltpu.with_memory_space_constraint(one, pltpu.HBM)


HBM = pl.BlockSpec(memory_space=pltpu.HBM)
DMA = pltpu.SemaphoreType.DMA


AXES = {"s": "span", "c": "chord", "n": "normal"}


def pairing(axis, start):
    count = lax.axis_size(axis)
    pairs = [(i, (i + 1) % count) for i in range(start, count, 2)]
    return pairs + [(j, i) for i, j in pairs]


def swap(*sends):
    got = []
    for at, one in enumerate(sends):
        name = "scn"[at // 2]
        got.append(lax.ppermute(one, AXES[name], pairing(AXES[name], at % 2)))
    return got


def owners():
    index = np.arange(256).reshape(16, 4, 2, 2)
    return index.transpose(1, 3, 0, 2).reshape(8, 32).tolist()


def ends(v):
    return (shape(v, 8, 128),) * 2 + (shape(v * 8, 128),) * 2 + (shape(8, 128),) * 2


def local(adjoint, jacobian, wall_table, face_type, mesh_map, stiffness, box_map, offsets):
    block = shape(3, CX, CY, CZ)
    out = call(edges_kernel, ends(5), (in_hbm(adjoint),), scratch=((5, CX, CY, CZ), DMA), remote=(0,))
    halo = swap(*out)
    fixed = (wall_table.transpose(1, 0, 2), mesh_map, adjoint, jacobian, face_type, stiffness)
    spaces = (pltpu.SMEM, pltpu.SMEM) + (pltpu.VMEM,) * 4
    start, *out = call(
        flux_kernel,
        (block, *ends(3)),
        (*map(in_hbm, fixed), *halo),
        scratch=(
            *(space(one.shape, one.dtype) for space, one in zip(spaces, fixed)),
            (5, CX, CY, CZ),
            (2, 5, 8, 128),
            (2, 40, 128),
            DMA((12,)),
        ),
        remote=range(6),
    )
    halo = swap(*out)
    kept = ((2, 3, 8, 128), (2, 24, 128))
    middle, *out = call(middle_kernel, (block, *ends(3)), (start, stiffness, *halo), scratch=kept)
    halo = swap(*out)
    bz, by, bx = tables()
    final, windows = call(
        window_kernel,
        (block, shape(WINDOWS, SLOT, 128)),
        (box_map.reshape(1), offsets.reshape(3), middle, start, stiffness, bz, by, bx, *halo),
        scratch=(*kept, (192, 128)),
        scalars=2,
    )
    got = lax.all_to_all(windows, ALL, 0, 0, axis_index_groups=owners(), tiled=True)
    keep, give = call(
        place_kernel,
        (shape(4, 72, 128),) * 2,
        (got.reshape(WINDOWS * SLOT, 128),),
        scratch=((3, 256, 512), (8, 72, 128)),
    )
    got = lax.ppermute(give, "normal", pairing("normal", 0))
    mine, *chunks = call(join_kernel, (shape(72, 128),) * 4, (keep, got))
    got = []
    for d, one in enumerate(chunks, 1):
        got.append(lax.ppermute(one, "chord", [(i, i ^ d) for i in range(4)]))
    grad = call(sum_kernel, shape(3, 1, 3072), (mine, *got), scratch=((72, 128),))
    return final, grad.reshape(1, 3, 3072)


def solution(mesh):
    placed = (
        P(None, "span", "chord", "normal"),
        P(None, None, None, "span", "chord", "normal"),
        P(),
        P("span", "chord"),
        P(),
        P(None, "span", "chord", "normal"),
        P("span", "chord", "normal"),
        P("span", "chord", "normal", None),
    )
    return jax.shard_map(
        local,
        mesh=mesh,
        in_specs=placed,
        out_specs=(P(None, "span", "chord", "normal"), P("span", None, ("chord", "normal"))),
        check_vma=False,
    )
```

```python
import math

import jax
import jax.numpy as jnp
import numpy as np
from jax import lax
from jax.experimental import pallas as pl
from jax.experimental.pallas import tpu as pltpu
from jax.sharding import PartitionSpec as P

F32 = jnp.float32
HIGHEST = lax.Precision.HIGHEST
ALL = ("span", "chord", "normal")
CX, CY, CZ = 8, 8, 128
LA = 96
ROWS = LA // 16
SLOT = 16
WINDOWS = 32


def bernstein(count, cells):
    degree = count - 1
    u = (np.arange(cells) + 0.5) / cells
    return np.stack([math.comb(degree, a) * u**a * (1 - u) ** (degree - a) for a in range(count)])


def tables():
    bx, by, bz = bernstein(8, CX), bernstein(8, CY), bernstein(8, CZ)
    along_z = np.zeros((CZ, 8, 2, 8))
    along_z[:] = bz.T[:, None, None, :]
    along_y = np.repeat(by.T, 16, axis=1)
    along_x = np.zeros((2, 4, 4, 3, CX, CY))
    for r in range(3):
        along_x[:, r, :, r] = 8.0 * bx.reshape(2, 4, CX)[..., None]
    return (
        along_z.reshape(CZ, 128).astype(np.float32),
        along_y.astype(np.float32),
        along_x.reshape(32, 192).astype(np.float32),
    )


def iotas():
    lane = lax.broadcasted_iota(jnp.int32, (8, 128), 1)
    row = lax.broadcasted_iota(jnp.int32, (8, 128), 0)
    return lane, row


def odd(axis):
    return lax.rem(lax.axis_index(axis), 2) == 1


def pick(flag, one, two):
    return jnp.where(jnp.full(one.shape, flag), one, two)


def pack(tile_of, fields, sends):
    lane, _ = iotas()
    xa, xb, ya, yb, za, zb = sends
    by_x, by_y, by_z = odd("span"), odd("chord"), odd("normal")
    low = jnp.zeros((8, 128), F32)
    high = jnp.zeros((8, 128), F32)
    for v in range(fields):
        first, last = tile_of(v, 0), tile_of(v, CX - 1)
        xa[v] = pick(by_x, first, last)
        xb[v] = pick(by_x, last, first)
        for x in range(CX):
            tile = tile_of(v, x)
            k = v * CX + x
            ya[k : k + 1, :] = pick(by_y, tile[0:1, :], tile[7:8, :])
            yb[k : k + 1, :] = pick(by_y, tile[7:8, :], tile[0:1, :])
            low = jnp.where(lane == k, pltpu.roll(tile, k, 1) if k else tile, low)
            high = jnp.where(lane == k, pltpu.roll(tile, k + 1, 1), high)
    za[...] = pick(by_z, low, high)
    zb[...] = pick(by_z, high, low)


def inner(axis, low, high):
    at = lax.axis_index(axis)
    last = lax.axis_size(axis) - 1
    zero = jnp.zeros(low.shape, F32)
    return pick(at > 0, low, zero), pick(at < last, high, zero)


def unpack(halo, planes_ref, rows_ref):
    xa, xb, ya, yb, za, zb = (one[...] for one in halo)
    by_x, by_y, by_z = odd("span"), odd("chord"), odd("normal")
    planes_ref[0], planes_ref[1] = inner("span", pick(by_x, xa, xb), pick(by_x, xb, xa))
    rows_ref[0], rows_ref[1] = inner("chord", pick(by_y, ya, yb), pick(by_y, yb, ya))
    return inner("normal", pick(by_z, za, zb), pick(by_z, zb, za))


def neighbour(e, tile_of, v, x, planes_ref, rows_ref, low, high):
    lane, row = iotas()
    k = v * CX + x
    if e == 1:
        return planes_ref[0, v] if x == 0 else tile_of(v, x - 1)
    if e == 2:
        return planes_ref[1, v] if x == CX - 1 else tile_of(v, x + 1)
    tile = tile_of(v, x)
    if e == 0:
        return tile
    if e == 3:
        return jnp.where(row == 0, rows_ref[0, k : k + 1, :], pltpu.roll(tile, 1, 0))
    if e == 4:
        return jnp.where(row == 7, rows_ref[1, k : k + 1, :], pltpu.roll(tile, 7, 0))
    if e == 5:
        return jnp.where(lane == 0, pltpu.roll(low, (128 - k) % 128, 1) if k else low, pltpu.roll(tile, 1, 1))
    return jnp.where(lane == 127, pltpu.roll(high, 127 - k, 1), pltpu.roll(tile, 127, 1))


def edges_kernel(adjoint_any, *refs):
    sends, (adjoint_ref, sem) = refs[:6], refs[6:]
    fetch = pltpu.make_async_copy(adjoint_any, adjoint_ref, sem)
    fetch.start()
    fetch.wait()
    pack(lambda v, x: adjoint_ref[v, x], 5, sends)


def flux_kernel(wall_any, map_any, adjoint_any, jacobian_any, face_any, stiff_any, *refs):
    halo, out_ref, sends = refs[:6], refs[6], refs[7:13]
    wall_ref, map_ref, adjoint_ref, jacobian_ref, face_ref, stiff_ref, total_ref, planes_ref, rows_ref, sems = refs[13:]
    copies = [
        pltpu.make_async_copy(wall_any, wall_ref, sems.at[0]),
        pltpu.make_async_copy(map_any, map_ref, sems.at[1]),
        pltpu.make_async_copy(adjoint_any, adjoint_ref, sems.at[2]),
        pltpu.make_async_copy(face_any, face_ref, sems.at[3]),
        pltpu.make_async_copy(stiff_any, stiff_ref, sems.at[4]),
    ]
    parts = [pltpu.make_async_copy(jacobian_any.at[e], jacobian_ref.at[e], sems.at[5 + e]) for e in range(7)]
    for copy in (copies[2], *parts, *copies[:2], copies[3], copies[4]):
        copy.start()
    lane, _ = iotas()
    on_wall = (lane == 0) & (lax.axis_index("normal") == 0)
    low, high = unpack(halo, planes_ref, rows_ref)
    tile_of = lambda v, x: adjoint_ref[v, x]
    copies[2].wait()
    for e in range(7):
        parts[e].wait()
        for x in range(CX):
            views = [neighbour(e, tile_of, p, x, planes_ref, rows_ref, low, high) for p in range(5)]
            total = [jnp.zeros((8, 128), F32) if e == 0 else total_ref[q, x] for q in range(5)]
            for p in range(5):
                for q in range(5):
                    total[q] = total[q] + jacobian_ref[e, p, q, x].astype(F32) * views[p]
            for q in range(5):
                total_ref[q, x] = total[q]
    for copy in (*copies[:2], *copies[3:]):
        copy.wait()
    square = lax.broadcasted_iota(jnp.int32, (8, 8), 0) == lax.broadcasted_iota(jnp.int32, (8, 8), 1)
    for x in range(CX):
        total = [total_ref[q, x] for q in range(5)]
        faces = jnp.broadcast_to(face_ref[x : x + 1, :], (8, 8)).astype(F32)
        face = jnp.sum(jnp.where(square, faces, 0.0), axis=1, keepdims=True)
        face = jnp.broadcast_to(face, (8, 128))
        for t in range(3):
            mask = on_wall & (face == float(t))
            for p in range(5):
                part = jnp.where(mask, adjoint_ref[p, x], 0.0)
                for q in range(5):
                    total[q] = total[q] + wall_ref[p, t, q] * part
        inverse = inverse_diagonal(stiff_ref, x)
        for r in range(3):
            sens = map_ref[r, 0] * total[0]
            for q in range(1, 5):
                sens = sens + map_ref[r, q] * total[q]
            out_ref[r, x] = sens * inverse
    pack(lambda v, x: out_ref[v, x], 3, sends)


def inverse_diagonal(stiff_ref, x):
    diagonal = stiff_ref[0, x]
    for e in range(1, 7):
        diagonal = diagonal + stiff_ref[e, x]
    return 1.0 / diagonal


def sweep(now_ref, start_ref, stiff_ref, halo, planes_ref, rows_ref, store):
    low, high = unpack(halo, planes_ref, rows_ref)
    tile_of = lambda v, x: now_ref[v, x]
    for x in range(CX):
        inverse = inverse_diagonal(stiff_ref, x)
        for v in range(3):
            total = stiff_ref[1, x] * neighbour(1, tile_of, v, x, planes_ref, rows_ref, low, high)
            for e in range(2, 7):
                total = total + stiff_ref[e, x] * neighbour(e, tile_of, v, x, planes_ref, rows_ref, low, high)
            store(v, x, start_ref[v, x] + total * inverse)


def middle_kernel(start_ref, stiff_ref, *refs):
    halo, out_ref, sends, planes_ref, rows_ref = refs[:6], refs[6], refs[7:13], *refs[13:]

    def store(v, x, tile):
        out_ref[v, x] = tile

    sweep(start_ref, start_ref, stiff_ref, halo, planes_ref, rows_ref, store)
    pack(lambda v, x: out_ref[v, x], 3, sends)


def window_kernel(box_ref, corner_ref, now_ref, start_ref, stiff_ref, bz_ref, by_ref, bx_ref, *refs):
    halo, out_ref, send_ref, planes_ref, rows_ref, flat_ref = refs[:6], *refs[6:]

    def store(v, x, tile):
        out_ref[v, x] = tile
        base = (v * CX + x) * CY
        flat_ref[base : base + CY, :] = tile

    sweep(now_ref, start_ref, stiff_ref, halo, planes_ref, rows_ref, store)
    inner = jnp.dot(flat_ref[...], bz_ref[...], precision=HIGHEST, preferred_element_type=F32)
    inner = inner * jnp.concatenate([by_ref[...]] * 24, axis=0)
    window = jnp.dot(bx_ref[...], inner, precision=HIGHEST, preferred_element_type=F32)
    lane = lax.broadcasted_iota(jnp.int32, (SLOT, 128), 1)
    row = lax.broadcasted_iota(jnp.int32, (SLOT, 128), 0)
    box = box_ref[0]
    oa, ob, oc = corner_ref[0], corner_ref[1], corner_ref[2]
    window = jnp.where(lax.rem(lane, 16) < 8, window[0:SLOT], window[SLOT : 2 * SLOT])
    shift = oc + 16 * lax.rem(ob, 8)
    window = pltpu.roll(window, shift, 1)
    inside = lax.rem(lane - shift + 128, 16) < 8
    block = jnp.where(inside, lax.div(ob, 8) + jnp.where(lane < shift, 1, 0), -1)
    there = jnp.where(row == 12, block, jnp.where(row == 13, oa, box)).astype(F32)
    there = jnp.where(row < 12, window, there)
    for at in range(WINDOWS):
        send_ref[at] = there


def split(one, count):
    parts = []
    for _ in range(count):
        part = one.astype(jnp.bfloat16)
        parts.append(part)
        one = one - part.astype(F32)
    return parts


def place_kernel(got_ref, *refs):
    keep_ref, give_ref, wide_ref, chunk_ref = refs
    half = lax.div(lax.axis_index("normal"), 2)
    span = lax.axis_index("span")
    nearest = lax.div(span, 8) * 8 + lax.rem(span, 2)
    where = got_ref[pl.ds(12, WINDOWS, stride=SLOT), :]
    start = got_ref[pl.ds(13, WINDOWS, stride=SLOT), :]
    lane = lax.broadcasted_iota(jnp.int32, (WINDOWS, 128), 1)
    row = lax.broadcasted_iota(jnp.int32, (WINDOWS, 128), 0)
    boxes = got_ref[pl.ds(14, WINDOWS, stride=SLOT), :]
    boxes = jnp.sum(jnp.where(lax.rem(lane, WINDOWS) == row, boxes, 0.0), axis=0, keepdims=True)
    start = jnp.sum(jnp.where(lax.rem(lane, WINDOWS) == row, start, 0.0), axis=0, keepdims=True)
    step = lax.div(lax.broadcasted_iota(jnp.int32, (1, 128), 1), WINDOWS).astype(F32)
    first = start + step
    line = lax.broadcasted_iota(jnp.int32, (64, 128), 0)
    chunk = lax.div(line, 8)
    owner = lax.axis_index("chord") * 4 + half * 2 + lax.rem(chunk, 2)
    same = (nearest + 2 * lax.div(chunk, 2)).astype(F32) == jnp.broadcast_to(boxes, (64, 128))
    point = jnp.where(lax.rem(line, 8) < ROWS, owner * ROWS + lax.rem(line, 8), -1).astype(F32)
    hits = jnp.concatenate(
        [jnp.where(same & (point == jnp.broadcast_to(first + 4.0 * h, (64, 128))), 1.0, 0.0) for h in range(2)], axis=1
    )
    hits = hits.astype(jnp.bfloat16)
    masks = [where == float(block) for block in range(4)]
    for r in range(3):
        for a in range(4):
            tile = got_ref[pl.ds(r * 4 + a, WINDOWS, stride=SLOT), :]
            for h in range(2):
                base = (h * 4 + a) * WINDOWS
                view = pltpu.roll(tile, 120, 1) if h else tile
                for block in range(4):
                    wide_ref[r, base : base + WINDOWS, block * 128 : block * 128 + 128] = jnp.where(
                        masks[block], view, 0.0
                    )
        placed = sum(jnp.dot(hits, part, preferred_element_type=F32) for part in split(wide_ref[r], 3))
        for i in range(8):
            for block in range(4):
                base = (r * 4 + block) * ROWS
                chunk_ref[i, base : base + ROWS, :] = placed[
                    i * 8 : i * 8 + ROWS, block * 128 : block * 128 + 128
                ]
    near = lax.rem(lax.axis_index("normal"), 2)
    for c in range(4):
        keep_ref[c] = chunk_ref[c * 2 + near]
        give_ref[c] = chunk_ref[c * 2 + 1 - near]


def join_kernel(keep_ref, got_ref, *sends):
    mine = lax.div(lax.rem(lax.axis_index("span"), 8), 2)
    for d in range(4):
        at = lax.bitwise_xor(mine, d)
        sends[d][...] = keep_ref[at] + got_ref[at]


def sum_kernel(*refs):
    got, (out_ref, total_ref) = refs[:4], refs[4:]
    total = got[0][...]
    for one in got[1:]:
        total = total + one[...]
    total_ref[...] = total
    for r in range(3):
        for block in range(4):
            for a in range(ROWS):
                base = a * 512 + block * 128
                at = (r * 4 + block) * ROWS + a
                out_ref[r, 0:1, base : base + 128] = total_ref[at : at + 1, :]


VMEM = pl.BlockSpec(memory_space=pltpu.VMEM)
SMEM = pl.BlockSpec(memory_space=pltpu.SMEM)


def shape(*dims):
    return jax.ShapeDtypeStruct(dims, F32)


def call(body, outs, ins, scratch=(), scalars=0, limit=24 << 20, remote=()):
    specs = [SMEM] * scalars + [VMEM] * (len(ins) - scalars)
    for at in remote:
        specs[at] = HBM
    return pl.pallas_call(
        body,
        out_shape=outs,
        in_specs=specs,
        out_specs=jax.tree.map(lambda _: VMEM, outs),
        scratch_shapes=[pltpu.VMEM(a, F32) if isinstance(a, tuple) else a for a in scratch],
        compiler_params=pltpu.CompilerParams(vmem_limit_bytes=limit),
    )(*ins)


def in_hbm(one):
    return pltpu.with_memory_space_constraint(one, pltpu.HBM)


HBM = pl.BlockSpec(memory_space=pltpu.HBM)
DMA = pltpu.SemaphoreType.DMA


AXES = {"s": "span", "c": "chord", "n": "normal"}


def pairing(axis, start):
    count = lax.axis_size(axis)
    pairs = [(i, (i + 1) % count) for i in range(start, count, 2)]
    return pairs + [(j, i) for i, j in pairs]


def swap(*sends):
    got = []
    for at, one in enumerate(sends):
        name = "scn"[at // 2]
        got.append(lax.ppermute(one, AXES[name], pairing(AXES[name], at % 2)))
    return got


def owners():
    index = np.arange(256).reshape(2, 4, 2, 4, 2, 2)
    return index.transpose(1, 5, 0, 2, 3, 4).reshape(8, 32).tolist()


def ends(v):
    return (shape(v, 8, 128),) * 2 + (shape(v * 8, 128),) * 2 + (shape(8, 128),) * 2


def local(adjoint, jacobian, wall_table, face_type, mesh_map, stiffness, box_map, offsets):
    block = shape(3, CX, CY, CZ)
    out = call(edges_kernel, ends(5), (in_hbm(adjoint),), scratch=((5, CX, CY, CZ), DMA), remote=(0,))
    halo = swap(*out)
    fixed = (wall_table.transpose(1, 0, 2), mesh_map, adjoint, jacobian, face_type, stiffness)
    spaces = (pltpu.SMEM, pltpu.SMEM) + (pltpu.VMEM,) * 4
    start, *out = call(
        flux_kernel,
        (block, *ends(3)),
        (*map(in_hbm, fixed), *halo),
        scratch=(
            *(space(one.shape, one.dtype) for space, one in zip(spaces, fixed)),
            (5, CX, CY, CZ),
            (2, 5, 8, 128),
            (2, 40, 128),
            DMA((12,)),
        ),
        remote=range(6),
    )
    halo = swap(*out)
    kept = ((2, 3, 8, 128), (2, 24, 128))
    middle, *out = call(middle_kernel, (block, *ends(3)), (start, stiffness, *halo), scratch=kept)
    halo = swap(*out)
    bz, by, bx = tables()
    final, windows = call(
        window_kernel,
        (block, shape(WINDOWS, SLOT, 128)),
        (box_map.reshape(1), offsets.reshape(3), middle, start, stiffness, bz, by, bx, *halo),
        scratch=(*kept, (192, 128)),
        scalars=2,
    )
    got = lax.all_to_all(windows, ALL, 0, 0, axis_index_groups=owners(), tiled=True)
    keep, give = call(
        place_kernel,
        (shape(4, 72, 128),) * 2,
        (got.reshape(WINDOWS * SLOT, 128),),
        scratch=((3, 256, 512), (8, 72, 128)),
    )
    got = lax.ppermute(give, "normal", pairing("normal", 0))
    mine, *chunks = call(join_kernel, (shape(72, 128),) * 4, (keep, got))
    got = []
    for d, one in enumerate(chunks, 1):
        got.append(lax.ppermute(one, "span", [(i, i ^ (2 * d)) for i in range(16)]))
    grad = call(sum_kernel, shape(3, 1, 3072), (mine, *got), scratch=((72, 128),))
    return final, grad.reshape(1, 3, 3072)


def solution(mesh):
    placed = (
        P(None, "span", "chord", "normal"),
        P(None, None, None, "span", "chord", "normal"),
        P(),
        P("span", "chord"),
        P(),
        P(None, "span", "chord", "normal"),
        P("span", "chord", "normal"),
        P("span", "chord", "normal", None),
    )
    return jax.shard_map(
        local,
        mesh=mesh,
        in_specs=placed,
        out_specs=(P(None, "span", "chord", "normal"), P("span", None, ("chord", "normal"))),
        check_vma=False,
    )
```

```python
import math

import jax
import jax.numpy as jnp
import numpy as np
from jax import lax
from jax.experimental import pallas as pl
from jax.experimental.pallas import tpu as pltpu
from jax.sharding import PartitionSpec as P

F32 = jnp.float32
HIGHEST = lax.Precision.HIGHEST
ALL = ("span", "chord", "normal")
CX, CY, CZ = 8, 8, 128
LA = 96
ROWS = LA // 16
SLOT = 16
WINDOWS = 32


def bernstein(count, cells):
    degree = count - 1
    u = (np.arange(cells) + 0.5) / cells
    return np.stack([math.comb(degree, a) * u**a * (1 - u) ** (degree - a) for a in range(count)])


def tables():
    bx, by, bz = bernstein(8, CX), bernstein(8, CY), bernstein(8, CZ)
    along_z = np.zeros((CZ, 8, 2, 8))
    along_z[:] = bz.T[:, None, None, :]
    along_y = np.repeat(by.T, 16, axis=1)
    along_x = np.zeros((2, 4, 4, 3, CX, CY))
    for r in range(3):
        along_x[:, r, :, r] = 8.0 * bx.reshape(2, 4, CX)[..., None]
    return (
        along_z.reshape(CZ, 128).astype(np.float32),
        along_y.astype(np.float32),
        along_x.reshape(32, 192).astype(np.float32),
    )


def iotas():
    lane = lax.broadcasted_iota(jnp.int32, (8, 128), 1)
    row = lax.broadcasted_iota(jnp.int32, (8, 128), 0)
    return lane, row


def odd(axis):
    return lax.rem(lax.axis_index(axis), 2) == 1


def pick(flag, one, two):
    return jnp.where(jnp.full(one.shape, flag), one, two)


def pack(tile_of, fields, sends):
    lane, _ = iotas()
    xa, xb, ya, yb, za, zb = sends
    by_x, by_y, by_z = odd("span"), odd("chord"), odd("normal")
    low = jnp.zeros((8, 128), F32)
    high = jnp.zeros((8, 128), F32)
    for v in range(fields):
        first, last = tile_of(v, 0), tile_of(v, CX - 1)
        xa[v] = pick(by_x, first, last)
        xb[v] = pick(by_x, last, first)
        for x in range(CX):
            tile = tile_of(v, x)
            k = v * CX + x
            ya[k : k + 1, :] = pick(by_y, tile[0:1, :], tile[7:8, :])
            yb[k : k + 1, :] = pick(by_y, tile[7:8, :], tile[0:1, :])
            low = jnp.where(lane == k, pltpu.roll(tile, k, 1) if k else tile, low)
            high = jnp.where(lane == k, pltpu.roll(tile, k + 1, 1), high)
    za[...] = pick(by_z, low, high)
    zb[...] = pick(by_z, high, low)


def inner(axis, low, high):
    at = lax.axis_index(axis)
    last = lax.axis_size(axis) - 1
    zero = jnp.zeros(low.shape, F32)
    return pick(at > 0, low, zero), pick(at < last, high, zero)


def unpack(halo, planes_ref, rows_ref):
    xa, xb, ya, yb, za, zb = (one[...] for one in halo)
    by_x, by_y, by_z = odd("span"), odd("chord"), odd("normal")
    planes_ref[0], planes_ref[1] = inner("span", pick(by_x, xa, xb), pick(by_x, xb, xa))
    rows_ref[0], rows_ref[1] = inner("chord", pick(by_y, ya, yb), pick(by_y, yb, ya))
    return inner("normal", pick(by_z, za, zb), pick(by_z, zb, za))


def neighbour(e, tile_of, v, x, planes_ref, rows_ref, low, high):
    lane, row = iotas()
    k = v * CX + x
    if e == 1:
        return planes_ref[0, v] if x == 0 else tile_of(v, x - 1)
    if e == 2:
        return planes_ref[1, v] if x == CX - 1 else tile_of(v, x + 1)
    tile = tile_of(v, x)
    if e == 0:
        return tile
    if e == 3:
        return jnp.where(row == 0, rows_ref[0, k : k + 1, :], pltpu.roll(tile, 1, 0))
    if e == 4:
        return jnp.where(row == 7, rows_ref[1, k : k + 1, :], pltpu.roll(tile, 7, 0))
    if e == 5:
        return jnp.where(lane == 0, pltpu.roll(low, (128 - k) % 128, 1) if k else low, pltpu.roll(tile, 1, 1))
    return jnp.where(lane == 127, pltpu.roll(high, 127 - k, 1), pltpu.roll(tile, 127, 1))


def edges_kernel(adjoint_any, *refs):
    sends, (adjoint_ref, sem) = refs[:6], refs[6:]
    fetch = pltpu.make_async_copy(adjoint_any, adjoint_ref, sem)
    fetch.start()
    fetch.wait()
    pack(lambda v, x: adjoint_ref[v, x], 5, sends)


def flux_kernel(wall_any, map_any, adjoint_any, jacobian_any, face_any, stiff_any, *refs):
    halo, out_ref, sends = refs[:6], refs[6], refs[7:13]
    wall_ref, map_ref, adjoint_ref, jacobian_ref, face_ref, stiff_ref, total_ref, planes_ref, rows_ref, sems = refs[13:]
    copies = [
        pltpu.make_async_copy(wall_any, wall_ref, sems.at[0]),
        pltpu.make_async_copy(map_any, map_ref, sems.at[1]),
        pltpu.make_async_copy(adjoint_any, adjoint_ref, sems.at[2]),
        pltpu.make_async_copy(face_any, face_ref, sems.at[3]),
        pltpu.make_async_copy(stiff_any, stiff_ref, sems.at[4]),
    ]
    parts = [pltpu.make_async_copy(jacobian_any.at[e], jacobian_ref.at[e], sems.at[5 + e]) for e in range(7)]
    for copy in (copies[2], *parts, *copies[:2], copies[3], copies[4]):
        copy.start()
    lane, _ = iotas()
    on_wall = (lane == 0) & (lax.axis_index("normal") == 0)
    low, high = unpack(halo, planes_ref, rows_ref)
    tile_of = lambda v, x: adjoint_ref[v, x]
    copies[2].wait()
    for e in range(7):
        parts[e].wait()
        for x in range(CX):
            views = [neighbour(e, tile_of, p, x, planes_ref, rows_ref, low, high) for p in range(5)]
            total = [jnp.zeros((8, 128), F32) if e == 0 else total_ref[q, x] for q in range(5)]
            for p in range(5):
                for q in range(5):
                    total[q] = total[q] + jacobian_ref[e, p, q, x].astype(F32) * views[p]
            for q in range(5):
                total_ref[q, x] = total[q]
    for copy in (*copies[:2], *copies[3:]):
        copy.wait()
    square = lax.broadcasted_iota(jnp.int32, (8, 8), 0) == lax.broadcasted_iota(jnp.int32, (8, 8), 1)
    for x in range(CX):
        total = [total_ref[q, x] for q in range(5)]
        faces = jnp.broadcast_to(face_ref[x : x + 1, :], (8, 8)).astype(F32)
        face = jnp.sum(jnp.where(square, faces, 0.0), axis=1, keepdims=True)
        face = jnp.broadcast_to(face, (8, 128))
        for t in range(3):
            mask = on_wall & (face == float(t))
            for p in range(5):
                part = jnp.where(mask, adjoint_ref[p, x], 0.0)
                for q in range(5):
                    total[q] = total[q] + wall_ref[p, t, q] * part
        inverse = inverse_diagonal(stiff_ref, x)
        for r in range(3):
            sens = map_ref[r, 0] * total[0]
            for q in range(1, 5):
                sens = sens + map_ref[r, q] * total[q]
            out_ref[r, x] = sens * inverse
    pack(lambda v, x: out_ref[v, x], 3, sends)


def inverse_diagonal(stiff_ref, x):
    diagonal = stiff_ref[0, x]
    for e in range(1, 7):
        diagonal = diagonal + stiff_ref[e, x]
    return 1.0 / diagonal


def sweep(now_ref, start_ref, stiff_ref, halo, planes_ref, rows_ref, store):
    low, high = unpack(halo, planes_ref, rows_ref)
    tile_of = lambda v, x: now_ref[v, x]
    for x in range(CX):
        inverse = inverse_diagonal(stiff_ref, x)
        for v in range(3):
            total = stiff_ref[1, x] * neighbour(1, tile_of, v, x, planes_ref, rows_ref, low, high)
            for e in range(2, 7):
                total = total + stiff_ref[e, x] * neighbour(e, tile_of, v, x, planes_ref, rows_ref, low, high)
            store(v, x, start_ref[v, x] + total * inverse)


def middle_kernel(start_ref, stiff_ref, *refs):
    halo, out_ref, sends, planes_ref, rows_ref = refs[:6], refs[6], refs[7:13], *refs[13:]

    def store(v, x, tile):
        out_ref[v, x] = tile

    sweep(start_ref, start_ref, stiff_ref, halo, planes_ref, rows_ref, store)
    pack(lambda v, x: out_ref[v, x], 3, sends)


def window_kernel(box_ref, corner_ref, now_ref, start_ref, stiff_ref, bz_ref, by_ref, bx_ref, *refs):
    halo, out_ref, send_ref, planes_ref, rows_ref, flat_ref = refs[:6], *refs[6:]

    def store(v, x, tile):
        out_ref[v, x] = tile
        base = (v * CX + x) * CY
        flat_ref[base : base + CY, :] = tile

    sweep(now_ref, start_ref, stiff_ref, halo, planes_ref, rows_ref, store)
    inner = jnp.dot(flat_ref[...], bz_ref[...], precision=HIGHEST, preferred_element_type=F32)
    inner = inner * jnp.concatenate([by_ref[...]] * 24, axis=0)
    window = jnp.dot(bx_ref[...], inner, precision=HIGHEST, preferred_element_type=F32)
    lane = lax.broadcasted_iota(jnp.int32, (SLOT, 128), 1)
    row = lax.broadcasted_iota(jnp.int32, (SLOT, 128), 0)
    box = box_ref[0]
    oa, ob, oc = corner_ref[0], corner_ref[1], corner_ref[2]
    window = jnp.where(lax.rem(lane, 16) < 8, window[0:SLOT], window[SLOT : 2 * SLOT])
    shift = oc + 16 * lax.rem(ob, 8)
    window = pltpu.roll(window, shift, 1)
    inside = lax.rem(lane - shift + 128, 16) < 8
    block = jnp.where(inside, lax.div(ob, 8) + jnp.where(lane < shift, 1, 0), -1)
    there = jnp.where(row == 12, block, jnp.where(row == 13, oa, box)).astype(F32)
    there = jnp.where(row < 12, window, there)
    for at in range(WINDOWS):
        send_ref[at] = there


def split(one, count):
    parts = []
    for _ in range(count):
        part = one.astype(jnp.bfloat16)
        parts.append(part)
        one = one - part.astype(F32)
    return parts


def place_kernel(got_ref, *refs):
    keep_ref, give_ref, wide_ref, chunk_ref = refs
    half = lax.div(lax.axis_index("normal"), 2)
    span = lax.axis_index("span")
    nearest = lax.div(span, 4) * 4
    where = got_ref[pl.ds(12, WINDOWS, stride=SLOT), :]
    start = got_ref[pl.ds(13, WINDOWS, stride=SLOT), :]
    lane = lax.broadcasted_iota(jnp.int32, (WINDOWS, 128), 1)
    row = lax.broadcasted_iota(jnp.int32, (WINDOWS, 128), 0)
    boxes = got_ref[pl.ds(14, WINDOWS, stride=SLOT), :]
    boxes = jnp.sum(jnp.where(lax.rem(lane, WINDOWS) == row, boxes, 0.0), axis=0, keepdims=True)
    start = jnp.sum(jnp.where(lax.rem(lane, WINDOWS) == row, start, 0.0), axis=0, keepdims=True)
    step = lax.div(lax.broadcasted_iota(jnp.int32, (1, 128), 1), WINDOWS).astype(F32)
    first = start + step
    line = lax.broadcasted_iota(jnp.int32, (64, 128), 0)
    chunk = lax.div(line, 8)
    owner = lax.axis_index("chord") * 4 + half * 2 + lax.rem(chunk, 2)
    same = (nearest + lax.div(chunk, 2)).astype(F32) == jnp.broadcast_to(boxes, (64, 128))
    point = jnp.where(lax.rem(line, 8) < ROWS, owner * ROWS + lax.rem(line, 8), -1).astype(F32)
    hits = jnp.concatenate(
        [jnp.where(same & (point == jnp.broadcast_to(first + 4.0 * h, (64, 128))), 1.0, 0.0) for h in range(2)], axis=1
    )
    hits = hits.astype(jnp.bfloat16)
    masks = [where == float(block) for block in range(4)]
    for r in range(3):
        for a in range(4):
            tile = got_ref[pl.ds(r * 4 + a, WINDOWS, stride=SLOT), :]
            for h in range(2):
                base = (h * 4 + a) * WINDOWS
                view = pltpu.roll(tile, 120, 1) if h else tile
                for block in range(4):
                    wide_ref[r, base : base + WINDOWS, block * 128 : block * 128 + 128] = jnp.where(
                        masks[block], view, 0.0
                    )
        placed = sum(jnp.dot(hits, part, preferred_element_type=F32) for part in split(wide_ref[r], 3))
        for i in range(8):
            for block in range(4):
                base = (r * 4 + block) * ROWS
                chunk_ref[i, base : base + ROWS, :] = placed[
                    i * 8 : i * 8 + ROWS, block * 128 : block * 128 + 128
                ]
    near = lax.rem(lax.axis_index("normal"), 2)
    for c in range(4):
        keep_ref[c] = chunk_ref[c * 2 + near]
        give_ref[c] = chunk_ref[c * 2 + 1 - near]


def join_kernel(keep_ref, got_ref, *sends):
    mine = lax.rem(lax.axis_index("span"), 4)
    for d in range(4):
        at = lax.bitwise_xor(mine, d)
        sends[d][...] = keep_ref[at] + got_ref[at]


def sum_kernel(*refs):
    got, (out_ref, total_ref) = refs[:4], refs[4:]
    total = got[0][...]
    for one in got[1:]:
        total = total + one[...]
    total_ref[...] = total
    for r in range(3):
        for block in range(4):
            for a in range(ROWS):
                base = a * 512 + block * 128
                at = (r * 4 + block) * ROWS + a
                out_ref[r, 0:1, base : base + 128] = total_ref[at : at + 1, :]


VMEM = pl.BlockSpec(memory_space=pltpu.VMEM)
SMEM = pl.BlockSpec(memory_space=pltpu.SMEM)


def shape(*dims):
    return jax.ShapeDtypeStruct(dims, F32)


def call(body, outs, ins, scratch=(), scalars=0, limit=24 << 20, remote=()):
    specs = [SMEM] * scalars + [VMEM] * (len(ins) - scalars)
    for at in remote:
        specs[at] = HBM
    return pl.pallas_call(
        body,
        out_shape=outs,
        in_specs=specs,
        out_specs=jax.tree.map(lambda _: VMEM, outs),
        scratch_shapes=[pltpu.VMEM(a, F32) if isinstance(a, tuple) else a for a in scratch],
        compiler_params=pltpu.CompilerParams(vmem_limit_bytes=limit),
    )(*ins)


def in_hbm(one):
    return pltpu.with_memory_space_constraint(one, pltpu.HBM)


HBM = pl.BlockSpec(memory_space=pltpu.HBM)
DMA = pltpu.SemaphoreType.DMA


AXES = {"s": "span", "c": "chord", "n": "normal"}


def pairing(axis, start):
    count = lax.axis_size(axis)
    pairs = [(i, (i + 1) % count) for i in range(start, count, 2)]
    return pairs + [(j, i) for i, j in pairs]


def swap(*sends):
    got = []
    for at, one in enumerate(sends):
        name = "scn"[at // 2]
        got.append(lax.ppermute(one, AXES[name], pairing(AXES[name], at % 2)))
    return got


def owners():
    index = np.arange(256).reshape(2, 2, 4, 4, 2, 2)
    return index.transpose(2, 5, 0, 1, 3, 4).reshape(8, 32).tolist()


def ends(v):
    return (shape(v, 8, 128),) * 2 + (shape(v * 8, 128),) * 2 + (shape(8, 128),) * 2


def local(adjoint, jacobian, wall_table, face_type, mesh_map, stiffness, box_map, offsets):
    block = shape(3, CX, CY, CZ)
    out = call(edges_kernel, ends(5), (in_hbm(adjoint),), scratch=((5, CX, CY, CZ), DMA), remote=(0,))
    halo = swap(*out)
    fixed = (wall_table.transpose(1, 0, 2), mesh_map, adjoint, jacobian, face_type, stiffness)
    spaces = (pltpu.SMEM, pltpu.SMEM) + (pltpu.VMEM,) * 4
    start, *out = call(
        flux_kernel,
        (block, *ends(3)),
        (*map(in_hbm, fixed), *halo),
        scratch=(
            *(space(one.shape, one.dtype) for space, one in zip(spaces, fixed)),
            (5, CX, CY, CZ),
            (2, 5, 8, 128),
            (2, 40, 128),
            DMA((12,)),
        ),
        remote=range(6),
    )
    halo = swap(*out)
    kept = ((2, 3, 8, 128), (2, 24, 128))
    middle, *out = call(middle_kernel, (block, *ends(3)), (start, stiffness, *halo), scratch=kept)
    halo = swap(*out)
    bz, by, bx = tables()
    final, windows = call(
        window_kernel,
        (block, shape(WINDOWS, SLOT, 128)),
        (box_map.reshape(1), offsets.reshape(3), middle, start, stiffness, bz, by, bx, *halo),
        scratch=(*kept, (192, 128)),
        scalars=2,
    )
    got = lax.all_to_all(windows, ALL, 0, 0, axis_index_groups=owners(), tiled=True)
    keep, give = call(
        place_kernel,
        (shape(4, 72, 128),) * 2,
        (got.reshape(WINDOWS * SLOT, 128),),
        scratch=((3, 256, 512), (8, 72, 128)),
    )
    got = lax.ppermute(give, "normal", pairing("normal", 0))
    mine, *chunks = call(join_kernel, (shape(72, 128),) * 4, (keep, got))
    got = []
    for d, one in enumerate(chunks, 1):
        got.append(lax.ppermute(one, "span", [(i, i ^ d) for i in range(16)]))
    grad = call(sum_kernel, shape(3, 1, 3072), (mine, *got), scratch=((72, 128),))
    return final, grad.reshape(1, 3, 3072)


def solution(mesh):
    placed = (
        P(None, "span", "chord", "normal"),
        P(None, None, None, "span", "chord", "normal"),
        P(),
        P("span", "chord"),
        P(),
        P(None, "span", "chord", "normal"),
        P("span", "chord", "normal"),
        P("span", "chord", "normal", None),
    )
    return jax.shard_map(
        local,
        mesh=mesh,
        in_specs=placed,
        out_specs=(P(None, "span", "chord", "normal"), P("span", None, ("chord", "normal"))),
        check_vma=False,
    )
```
